32 devices in a mesh: dp: 16 (over z, x, core), tensor: 2 (over y).
Axes of the slice: x: 2, y: 2, z: 4, core: 2. Of those that a mesh axis runs over, the one named last changes fastest.
Arguments:
- tokens: bfloat16 [16, 512, 1152], P('dp', 'tensor'), may hold values from -6 to 6
- text: bfloat16 [16, 120, 1152], P('dp', None, 'tensor'), may hold values from -6 to 6
- lengths: int32 [16], P('dp'), may hold values from 1 to 120, as said below
- modulation: float32 [16, 2, 6, 1152], P('dp'), may hold values from -1.5 to 1.5
- self_qkv: bfloat16 [2, 1152, 3, 1152], P(None, 'dp', None, 'tensor'), may hold values from -0.1875 to 0.1875
- self_out: bfloat16 [2, 1152, 1152], P(None, 'tensor', 'dp'), may hold values from -0.375 to 0.375
- cross_query: bfloat16 [2, 1152, 1152], P(None, 'dp', 'tensor'), may hold values from -0.1875 to 0.1875
- cross_keyvalue: bfloat16 [2, 1152, 2, 1152], P(None, 'dp', None, 'tensor'), may hold values from -0.1875 to 0.1875
- cross_out: bfloat16 [2, 1152, 1152], P(None, 'tensor', 'dp'), may hold values from -0.375 to 0.375
- mlp_in: bfloat16 [2, 1152, 4608], P(None, 'dp', 'tensor'), may hold values from -0.1875 to 0.1875
- mlp_out: bfloat16 [2, 4608, 1152], P(None, 'tensor', 'dp'), may hold values from -0.09375 to 0.09375
- cotangent: bfloat16 [16, 512, 1152], P('dp', 'tensor'), may hold values from -6 to 6
Outputs:
- output: bfloat16 [16, 512, 1152], P('dp', 'tensor')
- tokens_grad: float32 [16, 512, 1152], P('dp', 'tensor')
- text_grad: float32 [16, 120, 1152], P('dp', None, 'tensor')
- modulation_grad: float32 [16, 2, 6, 1152], P('dp')
- self_qkv_grad: float32 [2, 1152, 3, 1152], P(None, 'dp', None, 'tensor')
- self_out_grad: float32 [2, 1152, 1152], P(None, 'tensor', 'dp')
- cross_query_grad: float32 [2, 1152, 1152], P(None, 'dp', 'tensor')
- cross_keyvalue_grad: float32 [2, 1152, 2, 1152], P(None, 'dp', None, 'tensor')
- cross_out_grad: float32 [2, 1152, 1152], P(None, 'tensor', 'dp')
- mlp_in_grad: float32 [2, 1152, 4608], P(None, 'dp', 'tensor')
- mlp_out_grad: float32 [2, 4608, 1152], P(None, 'tensor', 'dp')
The draws below stay inside these ranges and needn't reach their ends.
Inputs may be any that keep to these rules, and one draw needn't show every extreme that they name: `lengths`: some clip has all 120 text tokens valid.
All inputs are finite; a program needn't handle non-finite values.
Results may differ from the reference program's by a relative error of at most 0.028.
Values may be sent and summed in bfloat16 or wider, within the bound.
No kernel may reach another device: no remote copies, remote signals or barrier semaphores. Data moves between devices by JAX's collectives and lax.ppermute only.
A program may use at most 256 MiB of HBM per device.

```python
import jax
import jax.numpy as jnp
from jax import lax

D = 1152
HEADS = 16
HEAD_DIM = 72
HID = 4608
TEXT = 120
PATCH = 256
LAYERS = 2
FRAMES = 2
CLIPS = 16


def draw_lengths(key, part):
    first, second = jax.random.split(key)
    counts = jax.random.randint(first, (CLIPS,), 1, TEXT + 1)
    chosen = jax.random.randint(second, (), 0, CLIPS)
    return jnp.where(jnp.arange(CLIPS) == chosen, TEXT, counts).astype(jnp.int32)


def draw_cotangent(key, part):
    first, second = jax.random.split(jax.random.fold_in(key, 7))
    noise = jax.random.normal(first, (CLIPS, FRAMES * PATCH, D), jnp.float32)
    common = 0.12 * jax.random.normal(second, (CLIPS, 1, D), jnp.float32)
    common = jnp.clip(common, -0.75, 0.75)
    return jnp.clip(noise + common, -6.0, 6.0).astype(jnp.bfloat16)


def levels(rng, dims, cuts, least, top_value):
    gain = 1.0
    for position, parts in cuts:
        steps = jax.random.uniform(jax.random.fold_in(jax.random.fold_in(rng, 6), position), (parts,), jnp.float32, least / len(cuts), top_value / len(cuts))
        gain = gain * jnp.repeat(jnp.exp(steps), dims[position] // parts).reshape((-1,) + (1,) * (len(dims) - 1 - position))
    return gain


def scatter_about(own_key, dims, scale, bound, cuts=(), dtype=jnp.bfloat16):
    level = levels(own_key, dims, cuts, -0.22, 0.18) if cuts else 1.0
    values = jax.random.normal(own_key, dims, jnp.float32) * scale * level
    return jnp.minimum(jnp.maximum(values, -bound), bound).astype(dtype)


def setup_inputs(seed: int = 0) -> dict:
    key_list = jax.random.split(jax.random.key(seed), 13)
    return {
        "tokens": scatter_about(key_list[0], (CLIPS, FRAMES * PATCH, D), 1.0, 6.0, ((0, 16), (1, 2))),
        "text": scatter_about(key_list[1], (CLIPS, TEXT, D), 1.0, 6.0, ((0, 16), (2, 2))),
        "lengths": draw_lengths(jax.random.fold_in(key_list[12], 71), 0),
        "modulation": scatter_about(key_list[3], (CLIPS, LAYERS, 6, D), 0.3, 1.5, ((0, 16),), jnp.float32),
        "self_qkv": scatter_about(key_list[4], (LAYERS, D, 3, D), D ** -0.5, 0.1875, ((1, 16), (3, 2))),
        "self_out": scatter_about(key_list[5], (LAYERS, D, D), (D // 4) ** -0.5, 0.375, ((1, 2), (2, 16))),
        "cross_query": scatter_about(key_list[6], (LAYERS, D, D), D ** -0.5, 0.1875, ((1, 16), (2, 2))),
        "cross_keyvalue": scatter_about(key_list[7], (LAYERS, D, 2, D), D ** -0.5, 0.1875, ((1, 16), (3, 2))),
        "cross_out": scatter_about(key_list[8], (LAYERS, D, D), (D // 4) ** -0.5, 0.375, ((1, 2), (2, 16))),
        "mlp_in": scatter_about(key_list[9], (LAYERS, D, HID), D ** -0.5, 0.1875, ((1, 16), (2, 2))),
        "mlp_out": scatter_about(key_list[10], (LAYERS, HID, D), HID ** -0.5, 0.09375, ((1, 2), (2, 16))),
        "cotangent": draw_cotangent(jax.random.fold_in(key_list[12], 71), 0),
    }


EPSILON = 1e-06
NEG_FILL = -1e+30

@jax.custom_vjp
def low(v):
    return lax.optimization_barrier(v.astype(jnp.bfloat16)).astype(jnp.float32)

@jax.custom_vjp
def low_back(v):
    return v

def low_keep(v):
    return (low(v), None)

def low_pass(kept, grad):
    return (grad,)

def back_keep(v):
    return (v, None)

def back_low(kept, grad):
    return (low(grad),)
low.defvjp(low_keep, low_pass)
low_back.defvjp(back_keep, back_low)

def rounded(value):
    return low(low_back(value))

def exact_dot(left, right):
    return jnp.dot(left, right, precision=lax.Precision.HIGHEST)

def norm_modulate(stream, shift, scale):
    center = stream - lax.optimization_barrier(jnp.mean(stream, axis=-1, keepdims=True))
    spread_sq = lax.optimization_barrier(jnp.mean(center * center, axis=-1, keepdims=True))
    return center * lax.rsqrt(spread_sq + EPSILON) * (1.0 + scale) + shift

def attend(queries, key_rows, values, visible):
    scores = jnp.einsum('glhe,gmhe->ghlm', queries, key_rows, precision=lax.Precision.HIGHEST)
    scores = low_back(scores * HEAD_DIM ** (-0.5))
    if visible is not None:
        scores = jnp.where(visible, scores, NEG_FILL)
    weights = low(jax.nn.softmax(scores, axis=-1))
    return rounded(jnp.einsum('ghlm,gmhe->glhe', weights, values, precision=lax.Precision.HIGHEST))

def to_groups(field, layer):
    grouped = field.reshape(FRAMES, PATCH, HEADS, HEAD_DIM)
    if layer % 2 == 1:
        grouped = grouped.transpose(1, 0, 2, 3)
    return grouped

def from_groups(field, layer):
    if layer % 2 == 1:
        field = field.transpose(1, 0, 2, 3)
    return field.reshape(FRAMES * PATCH, HEADS * HEAD_DIM)

def clip_forward(stream, text_low, modul, length, weights):
    self_qkv, self_out, cross_query, cross_keyvalue, cross_out, mlp_in, mlp_out = weights
    visible = jnp.arange(TEXT) < length
    for layer in range(LAYERS):
        adaln = modul[layer]
        normed = low(norm_modulate(stream, adaln[0], adaln[1]))
        qkv_rows = rounded(jnp.einsum('sd,dtc->stc', normed, self_qkv[layer], precision=lax.Precision.HIGHEST))
        queries = to_groups(qkv_rows[:, 0], layer)
        key_rows = to_groups(qkv_rows[:, 1], layer)
        values = to_groups(qkv_rows[:, 2], layer)
        attended = from_groups(attend(queries, key_rows, values, None), layer)
        stream = stream + adaln[2] * low_back(exact_dot(attended, self_out[layer]))
        crossing = low(stream)
        cross_q = rounded(exact_dot(crossing, cross_query[layer])).reshape(1, FRAMES * PATCH, HEADS, HEAD_DIM)
        text_kv = rounded(jnp.einsum('nd,dtc->ntc', text_low, cross_keyvalue[layer], precision=lax.Precision.HIGHEST))
        text_keys = text_kv[:, 0].reshape(1, TEXT, HEADS, HEAD_DIM)
        text_values = text_kv[:, 1].reshape(1, TEXT, HEADS, HEAD_DIM)
        cross_att = attend(cross_q, text_keys, text_values, visible).reshape(FRAMES * PATCH, D)
        stream = stream + low_back(exact_dot(cross_att, cross_out[layer]))
        inner = low(norm_modulate(stream, adaln[3], adaln[4]))
        hidden_pre = low_back(exact_dot(inner, mlp_in[layer]))
        hidden = low(jax.nn.gelu(hidden_pre, approximate=True))
        stream = stream + adaln[5] * low_back(exact_dot(hidden, mlp_out[layer]))
    return stream

def reference(tokens, text, lengths, modulation, self_qkv, self_out, cross_query, cross_keyvalue, cross_out, mlp_in, mlp_out, cotangent):
    stepper = jax.checkpoint(clip_forward)

    def forward(tokens_f, text_f, modul_f, qkv_f, proj_f, query_f, keyval_f, cout_f, fcin_f, fcout_f):
        text_low = low(text_f)
        weights = (qkv_f, proj_f, query_f, keyval_f, cout_f, fcin_f, fcout_f)

        def scan_step(carry, items):
            stream, text_clip, modul, length = items
            return (carry, stepper(stream, text_clip, modul, length, weights))
        return lax.scan(scan_step, jnp.zeros((), jnp.float32), (tokens_f, text_low, modul_f, lengths))[1]
    inputs = tuple((member.astype(jnp.float32) for member in (tokens, text, modulation, self_qkv, self_out, cross_query, cross_keyvalue, cross_out, mlp_in, mlp_out)))
    result, backward = jax.vjp(forward, *inputs)
    grads = backward(cotangent.astype(jnp.float32))
    return (result.astype(jnp.bfloat16), grads[0], grads[1], grads[2], grads[3], grads[4], grads[5], grads[6], grads[7], grads[8], grads[9])
```

```python
import jax
import jax.numpy as jnp
from jax import lax
from jax.sharding import PartitionSpec as P

HEADS = 16
HEAD_DIM = 72
TEXT = 120
PATCH = 256
LAYERS = 2
LANES = 128

EPSILON = 1e-06
NEG_FILL = -1e30
F32 = jnp.float32
BF16 = jnp.bfloat16


def normalize(stream):
    center = stream - jnp.mean(stream, axis=-1, keepdims=True)
    root = lax.rsqrt(jnp.mean(center * center, axis=-1, keepdims=True) + EPSILON)
    return (center * root, root)


def norm_back(grad, unit, root):
    return root * (
        grad
        - jnp.mean(grad, axis=-1, keepdims=True)
        - unit * jnp.mean(grad * unit, axis=-1, keepdims=True)
    )


def gelu_tanh(field):
    return jax.nn.gelu(field, approximate=True)


def dot(left, right, contract=((1,), (0,))):
    return lax.dot_general(left, right, (contract, ((), ())), preferred_element_type=F32)


def attend_forward(queries, key_rows, values, visible, scaling):
    scores = (
        jnp.einsum("glhe,gmhe->ghlm", queries, key_rows, preferred_element_type=F32) * scaling
    )
    if visible is not None:
        scores = jnp.where(visible, scores, NEG_FILL)
    log_total = jax.nn.logsumexp(scores, axis=-1)
    weights = jnp.exp(scores - log_total[..., None]).astype(BF16)
    result = jnp.einsum("ghlm,gmhe->glhe", weights, values, preferred_element_type=F32)
    return (result.astype(BF16), log_total)


def attend_back(queries, key_rows, values, visible, scaling, log_total, grad_out):
    scores = (
        jnp.einsum("glhe,gmhe->ghlm", queries, key_rows, preferred_element_type=F32) * scaling
    )
    if visible is not None:
        scores = jnp.where(visible, scores, NEG_FILL)
    probs = jnp.exp(scores - log_total[..., None])
    grad_probs = jnp.einsum("glhe,gmhe->ghlm", grad_out, values, preferred_element_type=F32)
    grad_values = jnp.einsum(
        "ghlm,glhe->gmhe", probs.astype(BF16), grad_out, preferred_element_type=F32
    )
    grad_scores = probs * (grad_probs - jnp.sum(probs * grad_probs, axis=-1, keepdims=True))
    grad_scores = grad_scores.astype(BF16)
    grad_queries = (
        jnp.einsum("ghlm,gmhe->glhe", grad_scores, key_rows, preferred_element_type=F32)
        * scaling
    )
    grad_keys = (
        jnp.einsum("ghlm,glhe->gmhe", grad_scores, queries, preferred_element_type=F32)
        * scaling
    )
    return (grad_queries.astype(BF16), grad_keys.astype(BF16), grad_values.astype(BF16))


def line_order(count):
    return list(range(0, count, 2)) + list(reversed(range(1, count, 2)))


class Layout:
    def __init__(self):
        self.tensor = lax.axis_size("tensor")
        self.dp = lax.axis_size("dp")
        self.core = 2
        self.far = 4
        self.near = self.dp // (self.core * self.far)
        self.far_order = line_order(self.far)
        self.near_order = line_order(self.near)
        self.tensor_order = line_order(self.tensor)

    def place(self, far, near, core):
        return (far * self.near + near) * self.core + core

    def hops(self, which):
        pairs = []
        for far in range(self.far):
            for near in range(self.near):
                for core in range(self.core):
                    here = self.place(far, near, core)
                    if which == "far":
                        spot = self.far_order.index(far)
                        there = (self.far_order[(spot + 1) % self.far], near, core)
                    elif which == "near":
                        spot = self.near_order.index(near)
                        there = (far, self.near_order[(spot + 1) % self.near], core)
                    else:
                        there = (far, near, 1 - core)
                    pairs.append((here, self.place(*there)))
        return pairs

    def send(self, field, which):
        if which == "tensor":
            count = self.tensor
            order = self.tensor_order
            pairs = [(order[i], order[(i + 1) % count]) for i in range(count)]
            return lax.ppermute(field, "tensor", pairs)
        return lax.ppermute(field, "dp", self.hops(which))

    def ring_gather(self, field, which, count):
        blocks = [field]
        for _ in range(count - 1):
            blocks.append(self.send(blocks[-1], which))
        return blocks

    def ring_sum(self, blocks, which):
        count = len(blocks)
        if count == 1:
            return blocks[0].astype(F32)
        moving = blocks[1].astype(BF16)
        for step in range(2, count):
            moving = (self.send(moving, which).astype(F32) + blocks[step].astype(F32)).astype(BF16)
        return self.send(moving, which).astype(F32) + blocks[0].astype(F32)

    def gather_rows(self, piece):
        near_in = jnp.concatenate(self.ring_gather(piece, "far", self.far), axis=0)
        mine = self.ring_gather(near_in, "near", self.near)
        others = [self.send(part, "core") for part in mine]
        return jnp.concatenate(mine + others, axis=0)

    def sum_rows(self, rows):
        half = rows.shape[0] // 2
        arrived = self.send(rows[half:], "core")
        rows = (rows[:half].astype(F32) + arrived.astype(F32)).astype(BF16)
        size = half // self.near
        blocks = [rows[i * size : (i + 1) * size] for i in range(self.near)]
        rows = self.ring_sum(blocks, "near").astype(BF16)
        size = size // self.far
        blocks = [rows[i * size : (i + 1) * size] for i in range(self.far)]
        return self.ring_sum(blocks, "far")

    def own_features(self, block, spot):
        me = lax.axis_index("dp")
        core = me % self.core
        near = (me // self.core) % self.near
        far = me // (self.core * self.near)

        def look(table, index):
            found = jnp.zeros_like(index)
            for place, value in enumerate(table):
                found = jnp.where(index == place, value, found)
            return found

        def spots(order):
            return [order.index(place) for place in range(len(order))]

        inner = spot % block
        which = spot // block
        far_step = which % self.far
        near_step = (which // self.far) % self.near
        core_step = which // (self.far * self.near)
        far_at = look(self.far_order, (look(spots(self.far_order), far) - far_step) % self.far)
        near_at = look(
            self.near_order, (look(spots(self.near_order), near) - near_step) % self.near
        )
        core_at = (core + core_step) % self.core
        return ((far_at * self.near + near_at) * self.core + core_at) * block + inner


def padded(width):
    return -(-width // LANES) * LANES


def widen(field):
    extra = padded(field.shape[-1]) - field.shape[-1]
    if extra == 0:
        return field
    return jnp.pad(field, [(0, 0)] * (field.ndim - 1) + [(0, extra)])


def per_device(
    tokens,
    text,
    lengths,
    modulation,
    self_qkv,
    self_out,
    cross_query,
    cross_keyvalue,
    cross_out,
    mlp_in,
    mlp_out,
    cotangent,
):
    lay = Layout()
    tensor_size = lay.tensor
    rows_here = tokens.shape[1]
    total_rows = rows_here * tensor_size
    frames_all = total_rows // PATCH
    heads_here = HEADS // tensor_size
    columns = heads_here * HEAD_DIM
    wide = padded(columns)
    width = tokens.shape[2]
    block = self_qkv.shape[1]
    scaling = HEAD_DIM ** (-0.5)
    me_tensor = lax.axis_index("tensor")
    visible = jnp.arange(TEXT) < lengths[0]

    spot = lax.broadcasted_iota(jnp.int32, (1, width), 1)
    wanted = lay.own_features(block, spot)
    feature = lax.broadcasted_iota(jnp.int32, (width, width), 0)
    order = (feature == wanted).astype(BF16)

    def exact(left, right, contract):
        return lax.dot_general(
            left,
            right.astype(left.dtype),
            (contract, ((), ())),
            precision=lax.Precision.HIGHEST,
            preferred_element_type=F32,
        )

    def into(field):
        if field.dtype == BF16:
            return dot(field, order)
        return exact(field, order, ((1,), (0,)))

    def back(field):
        if field.dtype == BF16:
            return dot(field, order, ((1,), (1,))).astype(BF16)
        return exact(field, order, ((1,), (1,)))

    def spread(field):
        return jnp.concatenate(lay.ring_gather(field, "tensor", tensor_size), axis=0)

    def collect(whole):
        return lay.ring_sum(
            [whole[i * rows_here : (i + 1) * rows_here] for i in range(tensor_size)], "tensor"
        )

    def fetch(layer):
        qkv = self_qkv[layer]
        keyval = cross_keyvalue[layer]
        first = jnp.concatenate(
            [widen(qkv[:, 0]), widen(qkv[:, 1]), widen(qkv[:, 2]), widen(self_out[layer].T)], axis=1
        )
        second = jnp.concatenate(
            [
                widen(cross_query[layer]),
                widen(keyval[:, 0]),
                widen(keyval[:, 1]),
                widen(cross_out[layer].T),
            ],
            axis=1,
        )
        return [lay.gather_rows(part) for part in (first, second, mlp_in[layer], mlp_out[layer].T)]

    def to_groups(field, layer):
        grouped = field.reshape(frames_all, PATCH, heads_here, HEAD_DIM)
        if layer % 2 == 1:
            grouped = grouped.transpose(1, 0, 2, 3)
        return grouped

    def from_groups(field, layer):
        if layer % 2 == 1:
            field = field.transpose(1, 0, 2, 3)
        return field.reshape(total_rows, columns)

    def piece(weight, index):
        return weight[:, index * wide : index * wide + columns]

    text_full = jnp.concatenate(
        [
            part
            for part in [lax.all_gather(text[0], "tensor", axis=1, tiled=True)]
        ],
        axis=1,
    )
    text_full = into(text_full).astype(BF16)
    table = into(modulation[0].reshape(LAYERS * 6, width)).reshape(LAYERS, 6, width)

    gathered = [fetch(layer) for layer in range(LAYERS)]

    stream = into(tokens[0])
    memory = []
    for layer in range(LAYERS):
        adaln = table[layer]
        first, second, weight_in, weight_out = gathered[layer]
        first_in = stream
        unit_one, root_one = normalize(first_in)
        normed_all = spread((unit_one * (1.0 + adaln[1]) + adaln[0]).astype(BF16))
        qkv_rows = [dot(normed_all, piece(first, i)).astype(BF16) for i in range(3)]
        queries, key_rows, values = [to_groups(part, layer) for part in qkv_rows]
        attended, log_self = attend_forward(queries, key_rows, values, None, scaling)
        attended = from_groups(attended, layer)
        branch = collect(dot(attended, piece(first, 3), ((1,), (1,))))
        second_in = first_in + adaln[2] * branch
        cross_all = spread(second_in.astype(BF16))
        cross_q = dot(cross_all, piece(second, 0)).astype(BF16)
        cross_q = cross_q.reshape(1, total_rows, heads_here, HEAD_DIM)
        text_keys = dot(text_full, piece(second, 1)).astype(BF16)
        text_values = dot(text_full, piece(second, 2)).astype(BF16)
        text_keys = text_keys.reshape(1, TEXT, heads_here, HEAD_DIM)
        text_values = text_values.reshape(1, TEXT, heads_here, HEAD_DIM)
        cross_att, log_cross = attend_forward(cross_q, text_keys, text_values, visible, scaling)
        cross_att = cross_att.reshape(total_rows, columns)
        crossed = collect(dot(cross_att, piece(second, 3), ((1,), (1,))))
        third_in = second_in + crossed
        unit_two, root_two = normalize(third_in)
        inner_all = spread((unit_two * (1.0 + adaln[4]) + adaln[3]).astype(BF16))
        hidden = gelu_tanh(dot(inner_all, weight_in)).astype(BF16)
        mlp_branch = collect(dot(hidden, weight_out, ((1,), (1,))))
        stream = third_in + adaln[5] * mlp_branch
        memory.append(
            (
                adaln,
                unit_one,
                root_one,
                normed_all,
                queries,
                key_rows,
                values,
                attended,
                log_self,
                branch,
                cross_all,
                cross_q,
                text_keys,
                text_values,
                cross_att,
                log_cross,
                unit_two,
                root_two,
                inner_all,
                mlp_branch,
            )
        )
    output = back(stream.astype(BF16))
    grad_stream = into(cotangent[0])
    grad_text = jnp.zeros((TEXT, width), F32)
    layer_grads = [None] * LAYERS
    table_rows = [None] * LAYERS
    for layer in reversed(range(LAYERS)):
        (
            adaln,
            unit_one,
            root_one,
            normed_all,
            queries,
            key_rows,
            values,
            attended,
            log_self,
            branch,
            cross_all,
            cross_q,
            text_keys,
            text_values,
            cross_att,
            log_cross,
            unit_two,
            root_two,
            inner_all,
            mlp_branch,
        ) = memory[layer]
        first, second, weight_in, weight_out = gathered[layer]
        rows_of = ((0,), (0,))
        over_columns = ((1,), (1,))

        grad_gate_two = jnp.sum(grad_stream * mlp_branch, axis=0)
        grad_mlp = spread((adaln[5] * grad_stream).astype(BF16))
        pre_mlp = dot(inner_all, weight_in)
        hidden_f, gelu_backward = jax.vjp(gelu_tanh, pre_mlp)
        hidden = hidden_f.astype(BF16)
        grad_hidden = dot(grad_mlp, weight_out)
        grad_pre = gelu_backward(grad_hidden)[0].astype(BF16)
        grad_inner = collect(dot(grad_pre, weight_in, over_columns))
        wide_out = lay.sum_rows(dot(grad_mlp, hidden, rows_of).astype(BF16))
        wide_in = lay.sum_rows(dot(inner_all, grad_pre, rows_of).astype(BF16))
        grad_shift_two = jnp.sum(grad_inner, axis=0)
        grad_scale_two = jnp.sum(grad_inner * unit_two, axis=0)
        grad_stream = grad_stream + norm_back(grad_inner * (1.0 + adaln[4]), unit_two, root_two)

        grad_crossed = spread(grad_stream.astype(BF16))
        grad_catt = dot(grad_crossed, piece(second, 3)).astype(BF16)
        grad_cq, grad_tkeys, grad_tvalues = attend_back(
            cross_q,
            text_keys,
            text_values,
            visible,
            scaling,
            log_cross,
            grad_catt.reshape(1, total_rows, heads_here, HEAD_DIM),
        )
        grad_cq = grad_cq.reshape(total_rows, columns)
        grad_tkeys = grad_tkeys.reshape(TEXT, columns)
        grad_tvalues = grad_tvalues.reshape(TEXT, columns)
        grad_stream = grad_stream + collect(dot(grad_cq, piece(second, 0), over_columns))
        grad_text = (
            grad_text
            + dot(grad_tkeys, piece(second, 1), over_columns)
            + dot(grad_tvalues, piece(second, 2), over_columns)
        )
        wide_second = lay.sum_rows(
            jnp.concatenate(
                [
                    widen(dot(cross_all, grad_cq, rows_of).astype(BF16)),
                    widen(dot(text_full, grad_tkeys, rows_of).astype(BF16)),
                    widen(dot(text_full, grad_tvalues, rows_of).astype(BF16)),
                    widen(dot(grad_crossed, cross_att, rows_of).astype(BF16)),
                ],
                axis=1,
            )
        )

        grad_gate_one = jnp.sum(grad_stream * branch, axis=0)
        grad_branch = spread((adaln[2] * grad_stream).astype(BF16))
        grad_att = to_groups(dot(grad_branch, piece(first, 3)).astype(BF16), layer)
        grads = attend_back(queries, key_rows, values, None, scaling, log_self, grad_att)
        grad_q, grad_k, grad_v = [from_groups(part, layer) for part in grads]
        partial = (
            dot(grad_q, piece(first, 0), over_columns)
            + dot(grad_k, piece(first, 1), over_columns)
            + dot(grad_v, piece(first, 2), over_columns)
        )
        grad_normed = collect(partial)
        wide_first = lay.sum_rows(
            jnp.concatenate(
                [
                    widen(dot(normed_all, grad_q, rows_of).astype(BF16)),
                    widen(dot(normed_all, grad_k, rows_of).astype(BF16)),
                    widen(dot(normed_all, grad_v, rows_of).astype(BF16)),
                    widen(dot(grad_branch, attended, rows_of).astype(BF16)),
                ],
                axis=1,
            )
        )
        grad_shift_one = jnp.sum(grad_normed, axis=0)
        grad_scale_one = jnp.sum(grad_normed * unit_one, axis=0)
        grad_stream = grad_stream + norm_back(grad_normed * (1.0 + adaln[1]), unit_one, root_one)
        table_rows[layer] = jnp.stack(
            [
                grad_shift_one,
                grad_scale_one,
                grad_gate_one,
                grad_shift_two,
                grad_scale_two,
                grad_gate_two,
            ]
        )
        layer_grads[layer] = (
            jnp.stack([piece(wide_first, i) for i in range(3)], axis=1),
            piece(wide_first, 3).T,
            piece(wide_second, 0),
            jnp.stack([piece(wide_second, i) for i in (1, 2)], axis=1),
            piece(wide_second, 3).T,
            wide_in,
            wide_out.T,
        )
    share = width // tensor_size
    grad_text = back(grad_text)
    text_grad = lax.psum_scatter(grad_text, "tensor", scatter_dimension=1, tiled=True)
    table_grad = back(
        lax.psum(jnp.stack(table_rows), "tensor").reshape(LAYERS * 6, width)
    ).reshape(LAYERS, 6, width)
    stacked = [
        jnp.stack([layer_grads[layer][member] for layer in range(LAYERS)]) for member in range(7)
    ]
    return (
        output[None],
        back(grad_stream)[None],
        text_grad[None],
        table_grad[None],
        *stacked,
    )


def solution(mesh):
    return jax.shard_map(
        per_device,
        mesh=mesh,
        in_specs=(
            P("dp", "tensor", None),
            P("dp", None, "tensor"),
            P("dp"),
            P("dp", None, None, None),
            P(None, "dp", None, "tensor"),
            P(None, "tensor", "dp"),
            P(None, "dp", "tensor"),
            P(None, "dp", None, "tensor"),
            P(None, "tensor", "dp"),
            P(None, "dp", "tensor"),
            P(None, "tensor", "dp"),
            P("dp", "tensor", None),
        ),
        out_specs=(
            P("dp", "tensor", None),
            P("dp", "tensor", None),
            P("dp", None, "tensor"),
            P("dp", None, None, None),
            P(None, "dp", None, "tensor"),
            P(None, "tensor", "dp"),
            P(None, "dp", "tensor"),
            P(None, "dp", None, "tensor"),
            P(None, "tensor", "dp"),
            P(None, "dp", "tensor"),
            P(None, "tensor", "dp"),
        ),
        check_vma=False,
    )
```

```python
import jax
import jax.numpy as jnp
from jax import lax
from jax.experimental import pallas as pl
from jax.experimental.pallas import tpu as pltpu
from jax.sharding import PartitionSpec as P

HEADS = 16
HEAD_DIM = 72
TEXT = 120
PATCH = 256
LAYERS = 2
LANES = 128

EPSILON = 1e-06
NEG_FILL = -1e30
F32 = jnp.float32
BF16 = jnp.bfloat16


def normalize(stream):
    center = stream - jnp.mean(stream, axis=-1, keepdims=True)
    root = lax.rsqrt(jnp.mean(center * center, axis=-1, keepdims=True) + EPSILON)
    return (center * root, root)


def norm_back(grad, unit, root):
    return root * (
        grad
        - jnp.mean(grad, axis=-1, keepdims=True)
        - unit * jnp.mean(grad * unit, axis=-1, keepdims=True)
    )


def gelu_tanh(field):
    return jax.nn.gelu(field, approximate=True)


def dot(left, right, contract=((1,), (0,))):
    return lax.dot_general(left, right, (contract, ((), ())), preferred_element_type=F32)


def padded(width):
    return -(-width // LANES) * LANES


def widen(field):
    extra = padded(field.shape[-1]) - field.shape[-1]
    if extra == 0:
        return field
    return jnp.pad(field, [(0, 0)] * (field.ndim - 1) + [(0, extra)])


def head_window(head):
    first = head * HEAD_DIM
    low = first // LANES * LANES
    high = padded(first + HEAD_DIM)
    lane = lax.broadcasted_iota(jnp.int32, (1, high - low), 1) + low
    return low, high, (lane >= first) & (lane < first + HEAD_DIM)


def hide(scores, limit_ref, period):
    if limit_ref is not None:
        key = lax.broadcasted_iota(jnp.int32, scores.shape, 1)
        return jnp.where(key < limit_ref[0], scores, NEG_FILL)
    if period is not None:
        row = lax.broadcasted_iota(jnp.int32, scores.shape, 0)
        key = lax.broadcasted_iota(jnp.int32, scores.shape, 1)
        return jnp.where(lax.rem(row, period) == lax.rem(key, period), scores, NEG_FILL)
    return scores


def attend_kernel(heads, period, limited, *refs):
    limit_ref = refs[0] if limited else None
    q_ref, k_ref, v_ref, out_ref, log_ref, held = refs[1 if limited else 0 :]
    scaling = HEAD_DIM ** (-0.5)
    held[...] = jnp.zeros_like(held)
    rows = held.shape[0]
    lane = lax.broadcasted_iota(jnp.int32, (rows, LANES), 1)
    logs = jnp.zeros((rows, LANES), F32)

    def take(ref, low, high):
        field = ref[:, :, low:high]
        return field.reshape(field.shape[0] * field.shape[1], high - low)

    for head in range(heads):
        low, high, inside = head_window(head)
        keep = inside.astype(F32).astype(BF16)
        scores = dot(take(q_ref, low, high) * keep, take(k_ref, low, high), ((1,), (1,)))
        scores = hide(scores * scaling, limit_ref, period)
        top = jnp.max(scores, axis=1, keepdims=True)
        weights = jnp.exp(scores - top)
        total = jnp.sum(weights, axis=1, keepdims=True)
        weights = (weights * (1.0 / total)).astype(BF16)
        result = dot(weights, take(v_ref, low, high))
        held[:, low:high] = jnp.where(inside, result, held[:, low:high])
        logs = jnp.where(lane == head, top + jnp.log(total), logs)
    out_ref[...] = held[...].astype(BF16).reshape(out_ref.shape)
    log_ref[...] = logs.reshape(log_ref.shape)


def attend_back_kernel(heads, period, limited, packed, *refs):
    limit_ref = refs[0] if limited else None
    refs = refs[1 if limited else 0 :]
    q_ref, k_ref, v_ref, grad_ref, log_ref, *outs, q_held, k_held, v_held = refs
    scaling = HEAD_DIM ** (-0.5)
    for held in (q_held, k_held, v_held):
        held[...] = jnp.zeros_like(held)
    rows = q_held.shape[0]
    lane = lax.broadcasted_iota(jnp.int32, (rows, LANES), 1)

    def take(ref, low, high):
        field = ref[:, :, low:high]
        return field.reshape(field.shape[0] * field.shape[1], high - low)

    for head in range(heads):
        low, high, inside = head_window(head)
        keep = inside.astype(F32).astype(BF16)
        queries = take(q_ref, low, high)
        keys = take(k_ref, low, high)
        grads = take(grad_ref, low, high)
        scores = dot(queries * keep, keys, ((1,), (1,))) * scaling
        scores = hide(scores, limit_ref, period)
        logs = jnp.where(lane == head, take(log_ref, 0, LANES), 0.0)
        probs = jnp.exp(scores - jnp.sum(logs, axis=1, keepdims=True))
        grad_probs = dot(grads * keep, take(v_ref, low, high), ((1,), (1,)))
        mean = jnp.sum(probs * grad_probs, axis=1, keepdims=True)
        grad_scores = (probs * (grad_probs - mean)).astype(BF16)
        first = ((0,), (0,))
        for held, value in (
            (q_held, dot(grad_scores, keys) * scaling),
            (k_held, dot(grad_scores, queries, first) * scaling),
            (v_held, dot(probs.astype(BF16), grads, first)),
        ):
            held[:, low:high] = jnp.where(inside, value, held[:, low:high])
    width = q_held.shape[1]
    query_out = outs[0]
    others = outs[0] if packed else outs[1]
    start = width if packed else 0
    spot = query_out.shape[:2] + (width,)
    query_out[:, :, :width] = q_held[...].astype(BF16).reshape(spot)
    spot = others.shape[:2] + (width,)
    others[:, :, start : start + width] = k_held[...].astype(others.dtype).reshape(spot)
    others[:, :, start + width :] = v_held[...].astype(others.dtype).reshape(spot)


def kernel_cost(units, heads, rows, keys, products):
    area = units * heads * rows * keys
    return pl.CostEstimate(
        flops=products * 2 * area * 256,
        transcendentals=area,
        bytes_accessed=units * (4 * rows + 2 * keys) * padded(heads * HEAD_DIM) * 2,
    )


def attend_parts(query, keyval, unit, heads):
    wide = padded(heads * HEAD_DIM)
    frames, rows = query.shape[:2]
    units = (frames // unit[0]) * (rows // unit[1])
    across = frames // unit[0]

    def at(u, column):
        return (u % across, u // across, column)

    own = pl.BlockSpec((*unit, wide), lambda u, *_: at(u, 0))
    if keyval is None:
        arrays = [query] * 3
        rest = [
            pl.BlockSpec((*unit, wide), lambda u, *_: at(u, 1)),
            pl.BlockSpec((*unit, wide), lambda u, *_: at(u, 2)),
        ]
        keys = unit[0] * unit[1]
    else:
        arrays = [query, keyval, keyval]
        keys = keyval.shape[1]
        rest = [
            pl.BlockSpec((1, keys, wide), lambda u, *_: (0, 0, 0)),
            pl.BlockSpec((1, keys, wide), lambda u, *_: (0, 0, 1)),
        ]
    logs = pl.BlockSpec((*unit, LANES), lambda u, *_: at(u, 0))
    packed = pl.BlockSpec((*unit, 3 * wide), lambda u, *_: at(u, 0))
    return arrays, [own, *rest], own, logs, packed, units, keys, wide


def attend(query, keyval, unit, heads, period=None, limit=None):
    arrays, specs, own, logs, _, units, keys, wide = attend_parts(query, keyval, unit, heads)
    limited = limit is not None
    rows = unit[0] * unit[1]
    return pl.pallas_call(
        lambda *refs: attend_kernel(heads, period, limited, *refs),
        out_shape=(
            jax.ShapeDtypeStruct((*query.shape[:2], wide), BF16),
            jax.ShapeDtypeStruct((*query.shape[:2], LANES), F32),
        ),
        grid_spec=pltpu.PrefetchScalarGridSpec(
            num_scalar_prefetch=1 if limited else 0,
            grid=(units,),
            in_specs=specs,
            out_specs=(own, logs),
            scratch_shapes=[pltpu.VMEM((rows, wide), F32)],
        ),
        cost_estimate=kernel_cost(units, heads, rows, keys, 2),
        name="attend",
    )(*([limit] if limited else []), *arrays)


def attend_back(query, keyval, grad, log, unit, heads, period=None, limit=None):
    arrays, specs, own, logs, packed, units, keys, wide = attend_parts(query, keyval, unit, heads)
    rows = unit[0] * unit[1]
    if keyval is None:
        out_shape = (jax.ShapeDtypeStruct(query.shape, BF16),)
        out_specs = (packed,)
    else:
        assert units == 1
        out_shape = (
            jax.ShapeDtypeStruct(query.shape, BF16),
            jax.ShapeDtypeStruct(keyval.shape, F32),
        )
        out_specs = (own, pl.BlockSpec((1, keys, 2 * wide), lambda u, *_: (0, 0, 0)))
    limited = limit is not None
    return pl.pallas_call(
        lambda *refs: attend_back_kernel(heads, period, limited, keyval is None, *refs),
        out_shape=out_shape,
        grid_spec=pltpu.PrefetchScalarGridSpec(
            num_scalar_prefetch=1 if limited else 0,
            grid=(units,),
            in_specs=[*specs, own, logs],
            out_specs=out_specs,
            scratch_shapes=[
                pltpu.VMEM((rows, wide), F32),
                pltpu.VMEM((keys, wide), F32),
                pltpu.VMEM((keys, wide), F32),
            ],
        ),
        cost_estimate=kernel_cost(units, heads, rows, keys, 5),
        name="attend_back",
    )(*([limit] if limited else []), *arrays, grad, log)


class Layout:
    def __init__(self):
        self.dp = lax.axis_size("dp")
        self.bits = self.dp.bit_length() - 1
        self.tensor = lax.axis_size("tensor")

    def send(self, field, bit):
        return lax.ppermute(field, "dp", [(place, place ^ (1 << bit)) for place in range(self.dp)])

    def shift(self, field, step):
        size = self.tensor
        return lax.ppermute(field, "tensor", [(i, (i + step) % size) for i in range(size)])

    def gathering(self, rows):
        for bit in range(self.bits - 1, -1, -1):
            rows = jnp.concatenate([rows] + (yield [(rows, bit)]), axis=0)
        return rows

    def summing(self, make):
        came = yield [(make(1).astype(BF16), 0)]
        rows = make(0) + came[0].astype(F32)
        for bit in range(1, self.bits):
            rows = rows.astype(BF16)
            half = rows.shape[0] // 2
            came = yield [(rows[half:], bit)]
            rows = rows[:half].astype(F32) + came[0].astype(F32)
        return rows

    def own_features(self, block, spot):
        which = spot // block
        place = jnp.zeros_like(which) + lax.axis_index("dp")
        for bit in range(self.bits):
            place = place ^ ((which >> bit & 1) << (self.bits - 1 - bit))
        return place * block + spot % block


def after(field, *others):
    return lax.optimization_barrier((field, *others))[0]


class Line:
    def __init__(self, send, patience):
        self.send = send
        self.patience = patience
        self.count = 0
        self.waiting = []
        self.moving = {}
        self.results = {}

    def add(self, name, begin, *fields):
        self.waiting.append((name, begin, fields))

    def resume(self, name, steps, came):
        try:
            return [(name, steps, steps.send(came))]
        except StopIteration as stop:
            self.results[name] = stop.value
            return []

    def depart(self, leaving):
        for name, steps, hops in leaving:
            due = self.count + 1 + self.patience.get(hops[0][1], 0)
            self.moving[name] = (steps, [self.send(*hop) for hop in hops], due)

    def step(self, field=None, exchange=None, starts=1):
        self.count += 1
        due = [name for name, entry in self.moving.items() if entry[2] <= self.count]
        begun = [self.waiting.pop(0) for _ in range(min(starts, len(self.waiting)))]
        flat = [block for name in due for block in self.moving[name][1]]
        flat += [block for *_, fields in begun for block in fields]
        if field is None:
            flat = list(lax.optimization_barrier(flat)) if flat else flat
        else:
            field, *flat = lax.optimization_barrier((field, *flat))
            came = exchange(field)
        leaving = []
        for name in due:
            steps, blocks, _ = self.moving.pop(name)
            leaving += self.resume(name, steps, [flat.pop(0) for _ in blocks])
        for name, begin, fields in begun:
            leaving += self.resume(name, begin(*[flat.pop(0) for _ in fields]), None)
        if field is not None:
            came = after(came, *[hop[0] for *_, hops in leaving for hop in hops])
        self.depart(leaving)
        return came if field is not None else None

    def need(self, name):
        while name not in self.results:
            steps, blocks, _ = self.moving.pop(name)
            self.depart(self.resume(name, steps, blocks))
        return self.results[name]

    def finish(self):
        while self.moving or self.waiting:
            leaving = []
            for name in list(self.moving):
                steps, blocks, _ = self.moving.pop(name)
                leaving += self.resume(name, steps, blocks)
            while self.waiting:
                name, begin, fields = self.waiting.pop(0)
                leaving += self.resume(name, begin(*fields), None)
            self.depart(leaving)


def per_device(
    tokens,
    text,
    lengths,
    modulation,
    self_qkv,
    self_out,
    cross_query,
    cross_keyvalue,
    cross_out,
    mlp_in,
    mlp_out,
    cotangent,
):
    lay = Layout()
    places = lay.tensor
    rows_here = tokens.shape[1]
    total_rows = rows_here * places
    heads_here = HEADS // places
    columns = heads_here * HEAD_DIM
    wide = padded(columns)
    width = tokens.shape[2]
    block = self_qkv.shape[1]
    me_tensor = lax.axis_index("tensor")
    share = width // places
    half = width // 2
    rows_of = ((0,), (0,))
    over_columns = ((1,), (1,))

    wanted = lay.own_features(block, lax.broadcasted_iota(jnp.int32, (1, width), 1))
    order = (lax.broadcasted_iota(jnp.int32, (width, width), 0) == wanted).astype(BF16)

    def share_order(step):
        first = (me_tensor - step) % places * share
        rows = lax.broadcasted_iota(jnp.int32, (share, width), 0) + first
        return (rows == wanted).astype(BF16)

    shares = [share_order(step) for step in range(places)]

    def exact(left, right, contract):
        return lax.dot_general(
            left,
            right.astype(F32),
            (contract, ((), ())),
            precision=lax.Precision.HIGHEST,
            preferred_element_type=F32,
        )

    def exchange(field, shift):
        starts = starts_at.get(line.count + 1, 0) if forward else 1
        return line.step(field, lambda f: lay.shift(f, shift), starts)

    def spread(field, timed=True):
        came = []
        for k in range(1, places):
            if timed and k == 1:
                came.append(exchange(field, 1))
            else:
                came.append(lay.shift(field, k))
        return [field, jnp.concatenate(came, axis=0) if len(came) > 1 else came[0]]

    def collect(parts):
        own, others = parts
        total = own
        for k in range(1, places):
            leaving = others[(k - 1) * rows_here : k * rows_here].astype(BF16)
            came = exchange(leaving, -1) if k == 1 else lay.shift(leaving, -k)
            total = total + came.astype(F32)
        return total

    def each(parts, weight, contract=((1,), (0,))):
        return [dot(part, weight, contract) for part in parts]

    def low(parts):
        return [part.astype(BF16) for part in parts]

    def join(parts):
        return jnp.concatenate(parts, axis=0)

    def split(field):
        return [field[:rows_here], field[rows_here:]]

    def pack(layer):
        qkv = self_qkv[layer]
        keyval = cross_keyvalue[layer]
        return {
            "qkv": jnp.concatenate([widen(qkv[:, i]) for i in range(3)], axis=1),
            "proj": widen(self_out[layer].T),
            "query": widen(cross_query[layer]),
            "keyval": jnp.concatenate([widen(keyval[:, i]) for i in range(2)], axis=1),
            "cproj": widen(cross_out[layer].T),
            "in": mlp_in[layer],
            "out": mlp_out[layer].T,
        }

    packs = [pack(layer) for layer in range(LAYERS)]
    groups = [
        (layer, names)
        for layer in range(LAYERS)
        for names in (("qkv", "proj"), ("query", "keyval", "cproj"), ("in",), ("out",))
    ]
    line = Line(lay.send, {1: 1})
    place_of = {}
    for index, (layer, names) in enumerate(groups):
        parts = [packs[layer][name] for name in names]
        piece = jnp.concatenate(parts, axis=1) if len(parts) > 1 else parts[0]
        line.add(index, lay.gathering, piece)
        start = 0
        for name, part in zip(names, parts):
            place_of[layer, name] = (index, start, start + part.shape[1])
            start += part.shape[1]
    starts_at = {6: 1, 8: 1, 9: 1, 10: 1, 12: 1}

    def weight(layer, name):
        index, start, stop = place_of[layer, name]
        return line.need(index)[:, start:stop]

    for starts in (1, 0, 1, 0, 1):
        line.step(starts=starts)

    text_rows = jnp.pad(text[0], ((0, LANES - TEXT), (0, 0)))
    text_full = sum(dot(part, at) for part, at in zip([text_rows] + [lay.shift(text_rows, k) for k in range(1, places)], shares))
    text_full = text_full.astype(BF16)
    table = exact(modulation[0].reshape(LAYERS * 6, width), order, ((1,), (0,)))
    table = table.reshape(LAYERS, 6, width)

    def frames(field):
        return field.reshape(-1, rows_here, field.shape[-1])

    def flat(field):
        return field.reshape(-1, field.shape[-1])

    def attend_self(layer, qkv):
        if layer % 2 == 0:
            found = [attend(frames(part), None, (1, rows_here), heads_here) for part in qkv]
            return [flat(one) for one, _ in found], [log for _, log in found]
        period = rows_here // places
        result, log = attend(frames(join(qkv)), None, (places, period), heads_here, period)
        return split(flat(result)), log

    def attend_self_back(layer, qkv, grad, log):
        if layer % 2 == 0:
            return [
                flat(attend_back(frames(a), None, frames(b), c, (1, rows_here), heads_here)[0])
                for a, b, c in zip(qkv, grad, log)
            ]
        period = rows_here // places
        (result,) = attend_back(
            frames(join(qkv)), None, frames(join(grad)), log, (places, period), heads_here, period
        )
        return split(flat(result))

    def attend_cross(queries, keyval):
        found = [
            attend(part[None], keyval[None], (1, part.shape[0]), heads_here, limit=lengths)
            for part in queries
        ]
        return [one[0] for one, _ in found], [log for _, log in found]

    def attend_cross_back(queries, keyval, grad, log):
        found = [
            attend_back(
                a[None], keyval[None], b[None], c, (1, a.shape[0]), heads_here, limit=lengths
            )
            for a, b, c in zip(queries, grad, log)
        ]
        return [one[0] for one, _ in found], sum(two[0] for _, two in found).astype(BF16)

    stream = dot(tokens[0], order)
    memory = []
    forward = True
    for layer in range(LAYERS):
        adaln = table[layer]
        save = {}
        save["unit_one"], save["root_one"] = normalize(stream)
        normed = spread(
            (save["unit_one"] * (1.0 + adaln[1]) + adaln[0]).astype(BF16), layer > 0
        )
        save["normed"] = join(normed)
        save["qkv"] = qkv = low(each(normed, weight(layer, "qkv")))
        attended, save["log_self"] = attend_self(layer, qkv)
        save["attended"] = join(attended)
        save["branch"] = branch = collect(each(attended, weight(layer, "proj"), over_columns))
        stream = stream + adaln[2] * branch
        crossing = spread(stream.astype(BF16))
        save["crossing"] = join(crossing)
        save["queries"] = queries = low(each(crossing, weight(layer, "query")))
        save["keyval"] = keyval = dot(text_full, weight(layer, "keyval")).astype(BF16)
        crossed, save["log_cross"] = attend_cross(queries, keyval)
        save["crossed"] = join(crossed)
        stream = stream + collect(each(crossed, weight(layer, "cproj"), over_columns))
        save["unit_two"], save["root_two"] = normalize(stream)
        inner = spread((save["unit_two"] * (1.0 + adaln[4]) + adaln[3]).astype(BF16))
        save["inner"] = join(inner)
        save["pre"] = pre = each(inner, weight(layer, "in"))
        hidden = low([gelu_tanh(part) for part in pre])
        save["hidden"] = join(hidden)
        save["mlp_branch"] = mlp_branch = collect(each(hidden, weight(layer, "out"), over_columns))
        stream = stream + adaln[5] * mlp_branch
        memory.append(save)
    output = dot(stream.astype(BF16), order, over_columns).astype(BF16)

    def product(*pairs):
        def make(which):
            made = [
                dot(left[:, which * half : (which + 1) * half], right, rows_of)
                for left, right in pairs
            ]
            return made[0] if len(made) == 1 else jnp.concatenate(made, axis=1)
        return lambda: lay.summing(make)

    weights = [
        {name: weight(layer, name) for spot, name in place_of if spot == layer}
        for layer in range(LAYERS)
    ]
    line = Line(lay.send, {1: 1})
    forward = False
    grad_stream = dot(cotangent[0], order)
    grad_text = jnp.zeros((LANES, width), F32)
    table_rows = [None] * LAYERS
    for layer in reversed(range(LAYERS)):
        adaln = table[layer]
        kind = weights[layer]
        save = memory[layer]

        grad_gate_two = jnp.sum(grad_stream * save["mlp_branch"], axis=0)
        grad_mlp = spread((adaln[5] * grad_stream).astype(BF16))
        line.add((layer, "out"), product((join(grad_mlp), save["hidden"])))
        grad_pre = [
            jax.vjp(gelu_tanh, pre)[1](dot(part, kind["out"]))[0].astype(BF16)
            for pre, part in zip(save["pre"], grad_mlp)
        ]
        line.add((layer, "in"), product((save["inner"], join(grad_pre))))
        grad_inner = collect(each(grad_pre, kind["in"], over_columns))
        grad_shift_two = jnp.sum(grad_inner, axis=0)
        grad_scale_two = jnp.sum(grad_inner * save["unit_two"], axis=0)
        grad_stream = grad_stream + norm_back(
            grad_inner * (1.0 + adaln[4]), save["unit_two"], save["root_two"]
        )

        grad_crossed = spread(grad_stream.astype(BF16))
        grad_catt = low(each(grad_crossed, kind["cproj"]))
        grad_cq, grad_keyval = attend_cross_back(
            save["queries"], save["keyval"], grad_catt, save["log_cross"]
        )
        line.add(
            (layer, "cross"),
            product(
                (save["crossing"], join(grad_cq)),
                (text_full, grad_keyval),
                (join(grad_crossed), save["crossed"]),
            ),
        )
        grad_stream = grad_stream + collect(each(grad_cq, kind["query"], over_columns))
        grad_text = grad_text + dot(grad_keyval, kind["keyval"], over_columns)

        grad_gate_one = jnp.sum(grad_stream * save["branch"], axis=0)
        grad_branch = spread((adaln[2] * grad_stream).astype(BF16))
        line.add((layer, "proj"), product((join(grad_branch), save["attended"])))
        grad_att = low(each(grad_branch, kind["proj"]))
        grad_qkv = attend_self_back(layer, save["qkv"], grad_att, save["log_self"])
        line.add(
            (layer, "self"),
            product((save["normed"], join(grad_qkv))),
        )
        grad_normed = collect(each(grad_qkv, kind["qkv"], over_columns))
        grad_shift_one = jnp.sum(grad_normed, axis=0)
        grad_scale_one = jnp.sum(grad_normed * save["unit_one"], axis=0)
        grad_stream = grad_stream + norm_back(
            grad_normed * (1.0 + adaln[1]), save["unit_one"], save["root_one"]
        )
        table_rows[layer] = jnp.stack(
            [
                grad_shift_one,
                grad_scale_one,
                grad_gate_one,
                grad_shift_two,
                grad_scale_two,
                grad_gate_two,
            ]
        )
    line.finish()

    def apart(field, first, count):
        return jnp.stack(
            [field[:, i * wide : i * wide + columns] for i in range(first, first + count)], axis=1
        )

    text_parts = [exact(grad_text[:TEXT], at, over_columns) for at in shares]
    text_grad = text_parts[0]
    for k in range(1, places):
        text_grad = text_grad + lay.shift(text_parts[k], -k)
    table_grad = exact(jnp.stack(table_rows).reshape(LAYERS * 6, width), order, over_columns)
    if places == 2:
        table_grad = table_grad + lay.shift(table_grad, 1)
    else:
        table_grad = lax.psum(table_grad, "tensor")
    selfs = [line.results[layer, "self"] for layer in range(LAYERS)]
    crosses = [line.results[layer, "cross"] for layer in range(LAYERS)]
    return (
        output[None],
        exact(grad_stream, order, over_columns)[None],
        text_grad[None],
        table_grad.reshape(LAYERS, 6, width)[None],
        jnp.stack([apart(one, 0, 3) for one in selfs]),
        jnp.stack([line.results[layer, "proj"][:, :columns].T for layer in range(LAYERS)]),
        jnp.stack([one[:, :columns] for one in crosses]),
        jnp.stack([apart(one, 1, 2) for one in crosses]),
        jnp.stack([one[:, 3 * wide : 3 * wide + columns].T for one in crosses]),
        jnp.stack([line.results[layer, "in"] for layer in range(LAYERS)]),
        jnp.stack([line.results[layer, "out"].T for layer in range(LAYERS)]),
    )


def solution(mesh):
    return jax.shard_map(
        per_device,
        mesh=mesh,
        in_specs=(
            P("dp", "tensor", None),
            P("dp", None, "tensor"),
            P("dp"),
            P("dp", None, None, None),
            P(None, "dp", None, "tensor"),
            P(None, "tensor", "dp"),
            P(None, "dp", "tensor"),
            P(None, "dp", None, "tensor"),
            P(None, "tensor", "dp"),
            P(None, "dp", "tensor"),
            P(None, "tensor", "dp"),
            P("dp", "tensor", None),
        ),
        out_specs=(
            P("dp", "tensor", None),
            P("dp", "tensor", None),
            P("dp", None, "tensor"),
            P("dp", None, None, None),
            P(None, "dp", None, "tensor"),
            P(None, "tensor", "dp"),
            P(None, "dp", "tensor"),
            P(None, "dp", None, "tensor"),
            P(None, "tensor", "dp"),
            P(None, "dp", "tensor"),
            P(None, "tensor", "dp"),
        ),
        check_vma=False,
    )
```

```python
import jax
import jax.numpy as jnp
from jax import lax
from jax.experimental import pallas as pl
from jax.experimental.pallas import tpu as pltpu
from jax.sharding import PartitionSpec as P

HEADS = 16
HEAD_DIM = 72
TEXT = 120
PATCH = 256
LAYERS = 2
LANES = 128

EPSILON = 1e-06
NEG_FILL = -1e30
F32 = jnp.float32
BF16 = jnp.bfloat16


def normalize(stream):
    center = stream - jnp.mean(stream, axis=-1, keepdims=True)
    root = lax.rsqrt(jnp.mean(center * center, axis=-1, keepdims=True) + EPSILON)
    return (center * root, root)


def norm_back(grad, unit, root):
    return root * (
        grad
        - jnp.mean(grad, axis=-1, keepdims=True)
        - unit * jnp.mean(grad * unit, axis=-1, keepdims=True)
    )


def gelu_tanh(field):
    return jax.nn.gelu(field, approximate=True)


def dot(left, right, contract=((1,), (0,))):
    return lax.dot_general(left, right, (contract, ((), ())), preferred_element_type=F32)


def padded(width):
    return -(-width // LANES) * LANES


def widen(field):
    extra = padded(field.shape[-1]) - field.shape[-1]
    if extra == 0:
        return field
    return jnp.pad(field, [(0, 0)] * (field.ndim - 1) + [(0, extra)])


def head_window(head):
    first = head * HEAD_DIM
    low = first // LANES * LANES
    high = padded(first + HEAD_DIM)
    lane = lax.broadcasted_iota(jnp.int32, (1, high - low), 1) + low
    return low, high, (lane >= first) & (lane < first + HEAD_DIM)


def hide(scores, limit_ref, period):
    if limit_ref is not None:
        key = lax.broadcasted_iota(jnp.int32, scores.shape, 1)
        return jnp.where(key < limit_ref[0], scores, NEG_FILL)
    if period is not None:
        row = lax.broadcasted_iota(jnp.int32, scores.shape, 0)
        key = lax.broadcasted_iota(jnp.int32, scores.shape, 1)
        return jnp.where(lax.rem(row, period) == lax.rem(key, period), scores, NEG_FILL)
    return scores


def attend_kernel(heads, period, limited, *refs):
    limit_ref = refs[0] if limited else None
    q_ref, k_ref, v_ref, out_ref, log_ref, held = refs[1 if limited else 0 :]
    scaling = HEAD_DIM ** (-0.5)
    held[...] = jnp.zeros_like(held)
    rows = held.shape[0]
    lane = lax.broadcasted_iota(jnp.int32, (rows, LANES), 1)
    logs = jnp.zeros((rows, LANES), F32)

    def take(ref, low, high):
        field = ref[:, :, low:high]
        return field.reshape(field.shape[0] * field.shape[1], high - low)

    for head in range(heads):
        low, high, inside = head_window(head)
        keep = inside.astype(F32).astype(BF16)
        scores = dot(take(q_ref, low, high) * keep, take(k_ref, low, high), ((1,), (1,)))
        scores = hide(scores * scaling, limit_ref, period)
        top = jnp.max(scores, axis=1, keepdims=True)
        weights = jnp.exp(scores - top)
        total = jnp.sum(weights, axis=1, keepdims=True)
        weights = (weights * (1.0 / total)).astype(BF16)
        result = dot(weights, take(v_ref, low, high))
        held[:, low:high] = jnp.where(inside, result, held[:, low:high])
        logs = jnp.where(lane == head, top + jnp.log(total), logs)
    out_ref[...] = held[...].astype(BF16).reshape(out_ref.shape)
    log_ref[...] = logs.reshape(log_ref.shape)


def attend_back_kernel(heads, period, limited, packed, *refs):
    limit_ref = refs[0] if limited else None
    refs = refs[1 if limited else 0 :]
    q_ref, k_ref, v_ref, grad_ref, log_ref, *outs, q_held, k_held, v_held = refs
    scaling = HEAD_DIM ** (-0.5)
    for held in (q_held, k_held, v_held):
        held[...] = jnp.zeros_like(held)
    rows = q_held.shape[0]
    lane = lax.broadcasted_iota(jnp.int32, (rows, LANES), 1)

    def take(ref, low, high):
        field = ref[:, :, low:high]
        return field.reshape(field.shape[0] * field.shape[1], high - low)

    for head in range(heads):
        low, high, inside = head_window(head)
        keep = inside.astype(F32).astype(BF16)
        queries = take(q_ref, low, high)
        keys = take(k_ref, low, high)
        grads = take(grad_ref, low, high)
        scores = dot(queries * keep, keys, ((1,), (1,))) * scaling
        scores = hide(scores, limit_ref, period)
        logs = jnp.where(lane == head, take(log_ref, 0, LANES), 0.0)
        probs = jnp.exp(scores - jnp.sum(logs, axis=1, keepdims=True))
        grad_probs = dot(grads * keep, take(v_ref, low, high), ((1,), (1,)))
        mean = jnp.sum(probs * grad_probs, axis=1, keepdims=True)
        grad_scores = (probs * (grad_probs - mean)).astype(BF16)
        first = ((0,), (0,))
        for held, value in (
            (q_held, dot(grad_scores, keys) * scaling),
            (k_held, dot(grad_scores, queries, first) * scaling),
            (v_held, dot(probs.astype(BF16), grads, first)),
        ):
            held[:, low:high] = jnp.where(inside, value, held[:, low:high])
    width = q_held.shape[1]
    query_out = outs[0]
    others = outs[0] if packed else outs[1]
    start = width if packed else 0
    spot = query_out.shape[:2] + (width,)
    query_out[:, :, :width] = q_held[...].astype(BF16).reshape(spot)
    spot = others.shape[:2] + (width,)
    others[:, :, start : start + width] = k_held[...].astype(others.dtype).reshape(spot)
    others[:, :, start + width :] = v_held[...].astype(others.dtype).reshape(spot)


def kernel_cost(units, heads, rows, keys, products):
    area = units * heads * rows * keys
    return pl.CostEstimate(
        flops=products * 2 * area * 256,
        transcendentals=area,
        bytes_accessed=units * (4 * rows + 2 * keys) * padded(heads * HEAD_DIM) * 2,
    )


def attend_parts(query, keyval, unit, heads):
    wide = padded(heads * HEAD_DIM)
    frames, rows = query.shape[:2]
    units = (frames // unit[0]) * (rows // unit[1])
    across = frames // unit[0]

    def at(u, column):
        return (u % across, u // across, column)

    own = pl.BlockSpec((*unit, wide), lambda u, *_: at(u, 0))
    if keyval is None:
        arrays = [query] * 3
        rest = [
            pl.BlockSpec((*unit, wide), lambda u, *_: at(u, 1)),
            pl.BlockSpec((*unit, wide), lambda u, *_: at(u, 2)),
        ]
        keys = unit[0] * unit[1]
    else:
        arrays = [query, keyval, keyval]
        keys = keyval.shape[1]
        rest = [
            pl.BlockSpec((1, keys, wide), lambda u, *_: (0, 0, 0)),
            pl.BlockSpec((1, keys, wide), lambda u, *_: (0, 0, 1)),
        ]
    logs = pl.BlockSpec((*unit, LANES), lambda u, *_: at(u, 0))
    packed = pl.BlockSpec((*unit, 3 * wide), lambda u, *_: at(u, 0))
    return arrays, [own, *rest], own, logs, packed, units, keys, wide


def attend(query, keyval, unit, heads, period=None, limit=None):
    arrays, specs, own, logs, _, units, keys, wide = attend_parts(query, keyval, unit, heads)
    limited = limit is not None
    rows = unit[0] * unit[1]
    return pl.pallas_call(
        lambda *refs: attend_kernel(heads, period, limited, *refs),
        out_shape=(
            jax.ShapeDtypeStruct((*query.shape[:2], wide), BF16),
            jax.ShapeDtypeStruct((*query.shape[:2], LANES), F32),
        ),
        grid_spec=pltpu.PrefetchScalarGridSpec(
            num_scalar_prefetch=1 if limited else 0,
            grid=(units,),
            in_specs=specs,
            out_specs=(own, logs),
            scratch_shapes=[pltpu.VMEM((rows, wide), F32)],
        ),
        cost_estimate=kernel_cost(units, heads, rows, keys, 2),
        name="attend",
    )(*([limit] if limited else []), *arrays)


def attend_back(query, keyval, grad, log, unit, heads, period=None, limit=None):
    arrays, specs, own, logs, packed, units, keys, wide = attend_parts(query, keyval, unit, heads)
    rows = unit[0] * unit[1]
    if keyval is None:
        out_shape = (jax.ShapeDtypeStruct(query.shape, BF16),)
        out_specs = (packed,)
    else:
        assert units == 1
        out_shape = (
            jax.ShapeDtypeStruct(query.shape, BF16),
            jax.ShapeDtypeStruct(keyval.shape, F32),
        )
        out_specs = (own, pl.BlockSpec((1, keys, 2 * wide), lambda u, *_: (0, 0, 0)))
    limited = limit is not None
    return pl.pallas_call(
        lambda *refs: attend_back_kernel(heads, period, limited, keyval is None, *refs),
        out_shape=out_shape,
        grid_spec=pltpu.PrefetchScalarGridSpec(
            num_scalar_prefetch=1 if limited else 0,
            grid=(units,),
            in_specs=[*specs, own, logs],
            out_specs=out_specs,
            scratch_shapes=[
                pltpu.VMEM((rows, wide), F32),
                pltpu.VMEM((keys, wide), F32),
                pltpu.VMEM((keys, wide), F32),
            ],
        ),
        cost_estimate=kernel_cost(units, heads, rows, keys, 5),
        name="attend_back",
    )(*([limit] if limited else []), *arrays, grad, log)


class Layout:
    def __init__(self):
        self.dp = lax.axis_size("dp")
        self.bits = self.dp.bit_length() - 1
        self.tensor = lax.axis_size("tensor")

    def send(self, field, bit):
        return lax.ppermute(field, "dp", [(place, place ^ (1 << bit)) for place in range(self.dp)])

    def shift(self, field, step):
        size = self.tensor
        return lax.ppermute(field, "tensor", [(i, (i + step) % size) for i in range(size)])

    def gathering(self, rows):
        for bit in range(self.bits - 1, -1, -1):
            rows = jnp.concatenate([rows] + (yield [(rows, bit)]), axis=0)
        return rows

    def summing(self, make):
        came = yield [(make(1).astype(BF16), 0)]
        rows = make(0) + came[0].astype(F32)
        for bit in range(1, self.bits):
            rows = rows.astype(BF16)
            half = rows.shape[0] // 2
            came = yield [(rows[half:], bit)]
            rows = rows[:half].astype(F32) + came[0].astype(F32)
        return rows

    def own_features(self, block, spot):
        which = spot // block
        place = jnp.zeros_like(which) + lax.axis_index("dp")
        for bit in range(self.bits):
            place = place ^ ((which >> bit & 1) << (self.bits - 1 - bit))
        return place * block + spot % block


def after(field, *others):
    return lax.optimization_barrier((field, *others))[0]


class Line:
    def __init__(self, send, patience):
        self.send = send
        self.patience = patience
        self.prompt = False
        self.count = 0
        self.ending = False
        self.last = None
        self.waiting = []
        self.moving = {}
        self.results = {}

    def add(self, name, begin, *fields):
        self.waiting.append((name, begin, fields))

    def resume(self, name, steps, came):
        try:
            return [(name, steps, steps.send(came))]
        except StopIteration as stop:
            self.results[name] = stop.value
            return []

    def depart(self, leaving):
        for name, steps, hops in leaving:
            due = self.count + 1 + self.patience.get(hops[0][1], 0)
            self.moving[name] = (steps, [self.send(*hop) for hop in hops], due)

    def step(self, field=None, exchange=None, starts=1):
        self.count += 1
        due = [name for name, entry in self.moving.items() if entry[2] <= self.count]
        begun = [self.waiting.pop(0) for _ in range(min(starts, len(self.waiting)))]
        flat = [block for name in due for block in self.moving[name][1]]
        flat += [block for *_, fields in begun for block in fields]
        if field is None:
            flat = list(lax.optimization_barrier(flat)) if flat else flat
        else:
            field, *flat = lax.optimization_barrier((field, *flat))
            came = exchange(field)
        leaving = []
        for name in due:
            steps, blocks, _ = self.moving.pop(name)
            leaving += self.resume(name, steps, [flat.pop(0) for _ in blocks])
        for name, begin, fields in begun:
            leaving += self.resume(name, begin(*[flat.pop(0) for _ in fields]), None)
        if field is not None:
            came = after(came, *[hop[0] for *_, hops in leaving for hop in hops])
        self.depart(leaving)
        if field is None:
            return None
        self.begun = [name for name, *_ in begun]
        for name, *_ in begun:
            if self.prompt:
                steps, blocks, due = self.moving[name]
                came, *blocks = lax.optimization_barrier((came, *blocks))
                self.moving[name] = (steps, blocks, due)
        self.last = came
        return came

    def hop(self, name, token):
        steps, blocks, _ = self.moving.pop(name)
        if token is not None:
            blocks = [after(block, token) for block in blocks]
        leaving = self.resume(name, steps, blocks)
        self.depart(leaving)
        return leaving[0][2][0][0] if leaving else self.results[name]

    def need(self, name):
        while name not in self.results:
            self.hop(name, self.last)
        return self.results[name]

    def finish(self):
        token = self.last
        for name in list(self.begun):
            token = self.hop(name, token)
        while self.moving:
            for name in list(self.moving):
                self.hop(name, token)


def per_device(
    tokens,
    text,
    lengths,
    modulation,
    self_qkv,
    self_out,
    cross_query,
    cross_keyvalue,
    cross_out,
    mlp_in,
    mlp_out,
    cotangent,
):
    lay = Layout()
    places = lay.tensor
    rows_here = tokens.shape[1]
    total_rows = rows_here * places
    heads_here = HEADS // places
    columns = heads_here * HEAD_DIM
    wide = padded(columns)
    width = tokens.shape[2]
    block = self_qkv.shape[1]
    me_tensor = lax.axis_index("tensor")
    share = width // places
    half = width // 2
    rows_of = ((0,), (0,))
    over_columns = ((1,), (1,))

    wanted = lay.own_features(block, lax.broadcasted_iota(jnp.int32, (1, width), 1))
    order = (lax.broadcasted_iota(jnp.int32, (width, width), 0) == wanted).astype(BF16)

    def share_order(step):
        first = (me_tensor - step) % places * share
        rows = lax.broadcasted_iota(jnp.int32, (share, width), 0) + first
        return (rows == wanted).astype(BF16)

    shares = [share_order(step) for step in range(places)]

    def exact(left, right, contract):
        return lax.dot_general(
            left,
            right.astype(F32),
            (contract, ((), ())),
            precision=lax.Precision.HIGHEST,
            preferred_element_type=F32,
        )

    def exchange(field, shift):
        starts = starts_at.get(line.count + 1, 0) if forward else 2 if line.ending else 1
        return line.step(field, lambda f: lay.shift(f, shift), starts)

    def spread(field, timed=True):
        came = []
        for k in range(1, places):
            if timed and k == 1:
                came.append(exchange(field, 1))
            else:
                came.append(lay.shift(field, k))
        return [field, jnp.concatenate(came, axis=0) if len(came) > 1 else came[0]]

    def collect(parts):
        own, others = parts
        total = own
        for k in range(1, places):
            leaving = others[(k - 1) * rows_here : k * rows_here].astype(BF16)
            came = exchange(leaving, -1) if k == 1 else lay.shift(leaving, -k)
            total = total + came.astype(F32)
        return total

    def each(parts, weight, contract=((1,), (0,))):
        return [dot(part, weight, contract) for part in parts]

    def low(parts):
        return [part.astype(BF16) for part in parts]

    def join(parts):
        return jnp.concatenate(parts, axis=0)

    def split(field):
        return [field[:rows_here], field[rows_here:]]

    def pack(layer):
        qkv = self_qkv[layer]
        keyval = cross_keyvalue[layer]
        return {
            "qkv": jnp.concatenate([widen(qkv[:, i]) for i in range(3)], axis=1),
            "proj": widen(self_out[layer].T),
            "query": widen(cross_query[layer]),
            "keyval": jnp.concatenate([widen(keyval[:, i]) for i in range(2)], axis=1),
            "cproj": widen(cross_out[layer].T),
            "in": mlp_in[layer],
            "out": mlp_out[layer].T,
        }

    packs = [pack(layer) for layer in range(LAYERS)]
    groups = [
        (layer, names)
        for layer in range(LAYERS)
        for names in (("qkv", "proj"), ("query", "keyval", "cproj"), ("in",), ("out",))
    ]
    line = Line(lay.send, {1: 1})
    place_of = {}
    for index, (layer, names) in enumerate(groups):
        parts = [packs[layer][name] for name in names]
        piece = jnp.concatenate(parts, axis=1) if len(parts) > 1 else parts[0]
        line.add(index, lay.gathering, piece)
        start = 0
        for name, part in zip(names, parts):
            place_of[layer, name] = (index, start, start + part.shape[1])
            start += part.shape[1]
    starts_at = {6: 1, 8: 1, 9: 1, 10: 1, 12: 1}

    def weight(layer, name):
        index, start, stop = place_of[layer, name]
        return line.need(index)[:, start:stop]

    for starts in (1, 0, 1, 0, 1):
        line.step(starts=starts)

    text_rows = jnp.pad(text[0], ((0, LANES - TEXT), (0, 0)))
    text_full = sum(dot(part, at) for part, at in zip([text_rows] + [lay.shift(text_rows, k) for k in range(1, places)], shares))
    text_full = text_full.astype(BF16)
    table = exact(modulation[0].reshape(LAYERS * 6, width), order, ((1,), (0,)))
    table = table.reshape(LAYERS, 6, width)

    def frames(field):
        return field.reshape(-1, rows_here, field.shape[-1])

    def flat(field):
        return field.reshape(-1, field.shape[-1])

    def attend_self(layer, qkv):
        if layer % 2 == 0:
            found = [attend(frames(part), None, (1, rows_here), heads_here) for part in qkv]
            return [flat(one) for one, _ in found], [log for _, log in found]
        period = rows_here // places
        result, log = attend(frames(join(qkv)), None, (places, period), heads_here, period)
        return split(flat(result)), log

    def attend_self_back(layer, qkv, grad, log):
        if layer % 2 == 0:
            return [
                flat(attend_back(frames(a), None, frames(b), c, (1, rows_here), heads_here)[0])
                for a, b, c in zip(qkv, grad, log)
            ]
        period = rows_here // places
        (result,) = attend_back(
            frames(join(qkv)), None, frames(join(grad)), log, (places, period), heads_here, period
        )
        return split(flat(result))

    def attend_cross(queries, keyval):
        found = [
            attend(part[None], keyval[None], (1, part.shape[0]), heads_here, limit=lengths)
            for part in queries
        ]
        return [one[0] for one, _ in found], [log for _, log in found]

    def attend_cross_back(queries, keyval, grad, log):
        found = [
            attend_back(
                a[None], keyval[None], b[None], c, (1, a.shape[0]), heads_here, limit=lengths
            )
            for a, b, c in zip(queries, grad, log)
        ]
        return [one[0] for one, _ in found], sum(two[0] for _, two in found).astype(BF16)

    stream = dot(tokens[0], order)
    memory = []
    forward = True
    for layer in range(LAYERS):
        adaln = table[layer]
        save = {}
        save["unit_one"], save["root_one"] = normalize(stream)
        normed = spread(
            (save["unit_one"] * (1.0 + adaln[1]) + adaln[0]).astype(BF16), layer > 0
        )
        save["normed"] = join(normed)
        save["qkv"] = qkv = low(each(normed, weight(layer, "qkv")))
        attended, save["log_self"] = attend_self(layer, qkv)
        save["attended"] = join(attended)
        save["branch"] = branch = collect(each(attended, weight(layer, "proj"), over_columns))
        stream = stream + adaln[2] * branch
        crossing = spread(stream.astype(BF16))
        save["crossing"] = join(crossing)
        save["queries"] = queries = low(each(crossing, weight(layer, "query")))
        save["keyval"] = keyval = dot(text_full, weight(layer, "keyval")).astype(BF16)
        crossed, save["log_cross"] = attend_cross(queries, keyval)
        save["crossed"] = join(crossed)
        stream = stream + collect(each(crossed, weight(layer, "cproj"), over_columns))
        save["unit_two"], save["root_two"] = normalize(stream)
        inner = spread((save["unit_two"] * (1.0 + adaln[4]) + adaln[3]).astype(BF16))
        save["inner"] = join(inner)
        save["pre"] = pre = each(inner, weight(layer, "in"))
        hidden = low([gelu_tanh(part) for part in pre])
        save["hidden"] = join(hidden)
        save["mlp_branch"] = mlp_branch = collect(each(hidden, weight(layer, "out"), over_columns))
        stream = stream + adaln[5] * mlp_branch
        memory.append(save)
    output = dot(stream.astype(BF16), order, over_columns).astype(BF16)

    def product(*pairs):
        def make(which):
            made = [
                dot(left[:, which * half : (which + 1) * half], right, rows_of)
                for left, right in pairs
            ]
            return made[0] if len(made) == 1 else jnp.concatenate(made, axis=1)
        return lambda: lay.summing(make)

    weights = [
        {name: weight(layer, name) for spot, name in place_of if spot == layer}
        for layer in range(LAYERS)
    ]
    line = Line(lay.send, {})
    line.prompt = True
    forward = False
    grad_stream = dot(cotangent[0], order)
    grad_text = jnp.zeros((LANES, width), F32)
    table_rows = [None] * LAYERS
    for layer in reversed(range(LAYERS)):
        adaln = table[layer]
        kind = weights[layer]
        save = memory[layer]

        grad_gate_two = jnp.sum(grad_stream * save["mlp_branch"], axis=0)
        grad_mlp = spread((adaln[5] * grad_stream).astype(BF16))
        line.add((layer, "out"), product((join(grad_mlp), save["hidden"])))
        grad_pre = [
            jax.vjp(gelu_tanh, pre)[1](dot(part, kind["out"]))[0].astype(BF16)
            for pre, part in zip(save["pre"], grad_mlp)
        ]
        line.add((layer, "in"), product((save["inner"], join(grad_pre))))
        grad_inner = collect(each(grad_pre, kind["in"], over_columns))
        grad_shift_two = jnp.sum(grad_inner, axis=0)
        grad_scale_two = jnp.sum(grad_inner * save["unit_two"], axis=0)
        grad_stream = grad_stream + norm_back(
            grad_inner * (1.0 + adaln[4]), save["unit_two"], save["root_two"]
        )

        grad_crossed = spread(grad_stream.astype(BF16))
        grad_catt = low(each(grad_crossed, kind["cproj"]))
        grad_cq, grad_keyval = attend_cross_back(
            save["queries"], save["keyval"], grad_catt, save["log_cross"]
        )
        line.add(
            (layer, "cross"),
            product(
                (save["crossing"], join(grad_cq)),
                (text_full, grad_keyval),
                (join(grad_crossed), save["crossed"]),
            ),
        )
        grad_stream = grad_stream + collect(each(grad_cq, kind["query"], over_columns))
        grad_text = grad_text + dot(grad_keyval, kind["keyval"], over_columns)

        grad_gate_one = jnp.sum(grad_stream * save["branch"], axis=0)
        grad_branch = spread((adaln[2] * grad_stream).astype(BF16))
        line.add((layer, "proj"), product((join(grad_branch), save["attended"])))
        grad_att = low(each(grad_branch, kind["proj"]))
        grad_qkv = attend_self_back(layer, save["qkv"], grad_att, save["log_self"])
        line.add(
            (layer, "self"),
            product((save["normed"], join(grad_qkv))),
        )
        line.ending = layer == 0
        grad_normed = collect(each(grad_qkv, kind["qkv"], over_columns))
        grad_shift_one = jnp.sum(grad_normed, axis=0)
        grad_scale_one = jnp.sum(grad_normed * save["unit_one"], axis=0)
        grad_stream = grad_stream + norm_back(
            grad_normed * (1.0 + adaln[1]), save["unit_one"], save["root_one"]
        )
        table_rows[layer] = jnp.stack(
            [
                grad_shift_one,
                grad_scale_one,
                grad_gate_one,
                grad_shift_two,
                grad_scale_two,
                grad_gate_two,
            ]
        )
    line.finish()

    def apart(field, first, count):
        return jnp.stack(
            [field[:, i * wide : i * wide + columns] for i in range(first, first + count)], axis=1
        )

    text_parts = [exact(grad_text[:TEXT], at, over_columns) for at in shares]
    text_grad = text_parts[0]
    for k in range(1, places):
        text_grad = text_grad + lay.shift(text_parts[k], -k)
    table_grad = exact(jnp.stack(table_rows).reshape(LAYERS * 6, width), order, over_columns)
    if places == 2:
        table_grad = table_grad + lay.shift(table_grad, 1)
    else:
        table_grad = lax.psum(table_grad, "tensor")
    selfs = [line.results[layer, "self"] for layer in range(LAYERS)]
    crosses = [line.results[layer, "cross"] for layer in range(LAYERS)]
    return (
        output[None],
        exact(grad_stream, order, over_columns)[None],
        text_grad[None],
        table_grad.reshape(LAYERS, 6, width)[None],
        jnp.stack([apart(one, 0, 3) for one in selfs]),
        jnp.stack([line.results[layer, "proj"][:, :columns].T for layer in range(LAYERS)]),
        jnp.stack([one[:, :columns] for one in crosses]),
        jnp.stack([apart(one, 1, 2) for one in crosses]),
        jnp.stack([one[:, 3 * wide : 3 * wide + columns].T for one in crosses]),
        jnp.stack([line.results[layer, "in"] for layer in range(LAYERS)]),
        jnp.stack([line.results[layer, "out"].T for layer in range(LAYERS)]),
    )


def solution(mesh):
    return jax.shard_map(
        per_device,
        mesh=mesh,
        in_specs=(
            P("dp", "tensor", None),
            P("dp", None, "tensor"),
            P("dp"),
            P("dp", None, None, None),
            P(None, "dp", None, "tensor"),
            P(None, "tensor", "dp"),
            P(None, "dp", "tensor"),
            P(None, "dp", None, "tensor"),
            P(None, "tensor", "dp"),
            P(None, "dp", "tensor"),
            P(None, "tensor", "dp"),
            P("dp", "tensor", None),
        ),
        out_specs=(
            P("dp", "tensor", None),
            P("dp", "tensor", None),
            P("dp", None, "tensor"),
            P("dp", None, None, None),
            P(None, "dp", None, "tensor"),
            P(None, "tensor", "dp"),
            P(None, "dp", "tensor"),
            P(None, "dp", None, "tensor"),
            P(None, "tensor", "dp"),
            P(None, "dp", "tensor"),
            P(None, "tensor", "dp"),
        ),
        check_vma=False,
    )
```

```python
import jax
import jax.numpy as jnp
from jax import lax
from jax.experimental import pallas as pl
from jax.experimental.pallas import tpu as pltpu
from jax.sharding import PartitionSpec as P

HEADS = 16
HEAD_DIM = 72
TEXT = 120
PATCH = 256
LAYERS = 2
LANES = 128

EPSILON = 1e-06
NEG_FILL = -1e30
F32 = jnp.float32
BF16 = jnp.bfloat16


def normalize(stream):
    center = stream - jnp.mean(stream, axis=-1, keepdims=True)
    root = lax.rsqrt(jnp.mean(center * center, axis=-1, keepdims=True) + EPSILON)
    return (center * root, root)


def norm_back(grad, unit, root):
    return root * (
        grad
        - jnp.mean(grad, axis=-1, keepdims=True)
        - unit * jnp.mean(grad * unit, axis=-1, keepdims=True)
    )


def gelu_tanh(field):
    return jax.nn.gelu(field, approximate=True)


def dot(left, right, contract=((1,), (0,))):
    return lax.dot_general(left, right, (contract, ((), ())), preferred_element_type=F32)


def padded(width):
    return -(-width // LANES) * LANES


def widen(field):
    extra = padded(field.shape[-1]) - field.shape[-1]
    if extra == 0:
        return field
    return jnp.pad(field, [(0, 0)] * (field.ndim - 1) + [(0, extra)])


def head_window(head):
    first = head * HEAD_DIM
    low = first // LANES * LANES
    high = padded(first + HEAD_DIM)
    lane = lax.broadcasted_iota(jnp.int32, (1, high - low), 1) + low
    return low, high, (lane >= first) & (lane < first + HEAD_DIM)


def hide(scores, limit_ref, period):
    if limit_ref is not None:
        key = lax.broadcasted_iota(jnp.int32, scores.shape, 1)
        return jnp.where(key < limit_ref[0], scores, NEG_FILL)
    if period is not None:
        row = lax.broadcasted_iota(jnp.int32, scores.shape, 0)
        key = lax.broadcasted_iota(jnp.int32, scores.shape, 1)
        return jnp.where(lax.rem(row, period) == lax.rem(key, period), scores, NEG_FILL)
    return scores


def attend_kernel(heads, period, limited, *refs):
    limit_ref = refs[0] if limited else None
    q_ref, k_ref, v_ref, out_ref, log_ref, held = refs[1 if limited else 0 :]
    scaling = HEAD_DIM ** (-0.5)
    held[...] = jnp.zeros_like(held)
    rows = held.shape[0]
    lane = lax.broadcasted_iota(jnp.int32, (rows, LANES), 1)
    logs = jnp.zeros((rows, LANES), F32)

    def take(ref, low, high):
        field = ref[:, :, low:high]
        return field.reshape(field.shape[0] * field.shape[1], high - low)

    for head in range(heads):
        low, high, inside = head_window(head)
        keep = inside.astype(F32).astype(BF16)
        scores = dot(take(q_ref, low, high) * keep, take(k_ref, low, high), ((1,), (1,)))
        scores = hide(scores * scaling, limit_ref, period)
        top = jnp.max(scores, axis=1, keepdims=True)
        weights = jnp.exp(scores - top)
        total = jnp.sum(weights, axis=1, keepdims=True)
        weights = (weights * (1.0 / total)).astype(BF16)
        result = dot(weights, take(v_ref, low, high))
        held[:, low:high] = jnp.where(inside, result, held[:, low:high])
        logs = jnp.where(lane == head, top + jnp.log(total), logs)
    out_ref[...] = held[...].astype(BF16).reshape(out_ref.shape)
    log_ref[...] = logs.reshape(log_ref.shape)


def attend_back_kernel(heads, period, limited, packed, *refs):
    limit_ref = refs[0] if limited else None
    refs = refs[1 if limited else 0 :]
    q_ref, k_ref, v_ref, grad_ref, log_ref, *outs, q_held, k_held, v_held = refs
    scaling = HEAD_DIM ** (-0.5)
    for held in (q_held, k_held, v_held):
        held[...] = jnp.zeros_like(held)
    rows = q_held.shape[0]
    lane = lax.broadcasted_iota(jnp.int32, (rows, LANES), 1)

    def take(ref, low, high):
        field = ref[:, :, low:high]
        return field.reshape(field.shape[0] * field.shape[1], high - low)

    for head in range(heads):
        low, high, inside = head_window(head)
        keep = inside.astype(F32).astype(BF16)
        queries = take(q_ref, low, high)
        keys = take(k_ref, low, high)
        grads = take(grad_ref, low, high)
        scores = dot(queries * keep, keys, ((1,), (1,))) * scaling
        scores = hide(scores, limit_ref, period)
        logs = jnp.where(lane == head, take(log_ref, 0, LANES), 0.0)
        probs = jnp.exp(scores - jnp.sum(logs, axis=1, keepdims=True))
        grad_probs = dot(grads * keep, take(v_ref, low, high), ((1,), (1,)))
        mean = jnp.sum(probs * grad_probs, axis=1, keepdims=True)
        grad_scores = (probs * (grad_probs - mean)).astype(BF16)
        first = ((0,), (0,))
        for held, value in (
            (q_held, dot(grad_scores, keys) * scaling),
            (k_held, dot(grad_scores, queries, first) * scaling),
            (v_held, dot(probs.astype(BF16), grads, first)),
        ):
            held[:, low:high] = jnp.where(inside, value, held[:, low:high])
    width = q_held.shape[1]
    query_out = outs[0]
    others = outs[0] if packed else outs[1]
    start = width if packed else 0
    spot = query_out.shape[:2] + (width,)
    query_out[:, :, :width] = q_held[...].astype(BF16).reshape(spot)
    spot = others.shape[:2] + (width,)
    others[:, :, start : start + width] = k_held[...].astype(others.dtype).reshape(spot)
    others[:, :, start + width :] = v_held[...].astype(others.dtype).reshape(spot)


def kernel_cost(units, heads, rows, keys, products):
    area = units * heads * rows * keys
    return pl.CostEstimate(
        flops=products * 2 * area * 256,
        transcendentals=area,
        bytes_accessed=units * (4 * rows + 2 * keys) * padded(heads * HEAD_DIM) * 2,
    )


def attend_parts(query, keyval, unit, heads):
    wide = padded(heads * HEAD_DIM)
    frames, rows = query.shape[:2]
    units = (frames // unit[0]) * (rows // unit[1])
    across = frames // unit[0]

    def at(u, column):
        return (u % across, u // across, column)

    own = pl.BlockSpec((*unit, wide), lambda u, *_: at(u, 0))
    if keyval is None:
        arrays = [query] * 3
        rest = [
            pl.BlockSpec((*unit, wide), lambda u, *_: at(u, 1)),
            pl.BlockSpec((*unit, wide), lambda u, *_: at(u, 2)),
        ]
        keys = unit[0] * unit[1]
    else:
        arrays = [query, keyval, keyval]
        keys = keyval.shape[1]
        rest = [
            pl.BlockSpec((1, keys, wide), lambda u, *_: (0, 0, 0)),
            pl.BlockSpec((1, keys, wide), lambda u, *_: (0, 0, 1)),
        ]
    logs = pl.BlockSpec((*unit, LANES), lambda u, *_: at(u, 0))
    packed = pl.BlockSpec((*unit, 3 * wide), lambda u, *_: at(u, 0))
    return arrays, [own, *rest], own, logs, packed, units, keys, wide


def attend(query, keyval, unit, heads, period=None, limit=None):
    arrays, specs, own, logs, _, units, keys, wide = attend_parts(query, keyval, unit, heads)
    limited = limit is not None
    rows = unit[0] * unit[1]
    return pl.pallas_call(
        lambda *refs: attend_kernel(heads, period, limited, *refs),
        out_shape=(
            jax.ShapeDtypeStruct((*query.shape[:2], wide), BF16),
            jax.ShapeDtypeStruct((*query.shape[:2], LANES), F32),
        ),
        grid_spec=pltpu.PrefetchScalarGridSpec(
            num_scalar_prefetch=1 if limited else 0,
            grid=(units,),
            in_specs=specs,
            out_specs=(own, logs),
            scratch_shapes=[pltpu.VMEM((rows, wide), F32)],
        ),
        cost_estimate=kernel_cost(units, heads, rows, keys, 2),
        name="attend",
    )(*([limit] if limited else []), *arrays)


def attend_back(query, keyval, grad, log, unit, heads, period=None, limit=None):
    arrays, specs, own, logs, packed, units, keys, wide = attend_parts(query, keyval, unit, heads)
    rows = unit[0] * unit[1]
    if keyval is None:
        out_shape = (jax.ShapeDtypeStruct(query.shape, BF16),)
        out_specs = (packed,)
    else:
        assert units == 1
        out_shape = (
            jax.ShapeDtypeStruct(query.shape, BF16),
            jax.ShapeDtypeStruct(keyval.shape, F32),
        )
        out_specs = (own, pl.BlockSpec((1, keys, 2 * wide), lambda u, *_: (0, 0, 0)))
    limited = limit is not None
    return pl.pallas_call(
        lambda *refs: attend_back_kernel(heads, period, limited, keyval is None, *refs),
        out_shape=out_shape,
        grid_spec=pltpu.PrefetchScalarGridSpec(
            num_scalar_prefetch=1 if limited else 0,
            grid=(units,),
            in_specs=[*specs, own, logs],
            out_specs=out_specs,
            scratch_shapes=[
                pltpu.VMEM((rows, wide), F32),
                pltpu.VMEM((keys, wide), F32),
                pltpu.VMEM((keys, wide), F32),
            ],
        ),
        cost_estimate=kernel_cost(units, heads, rows, keys, 5),
        name="attend_back",
    )(*([limit] if limited else []), *arrays, grad, log)


class Layout:
    def __init__(self):
        self.dp = lax.axis_size("dp")
        self.bits = self.dp.bit_length() - 1
        self.tensor = lax.axis_size("tensor")

    def send(self, field, bit):
        return lax.ppermute(field, "dp", [(place, place ^ (1 << bit)) for place in range(self.dp)])

    def shift(self, field, step):
        size = self.tensor
        return lax.ppermute(field, "tensor", [(i, (i + step) % size) for i in range(size)])

    def gathering(self, rows):
        for bit in range(self.bits - 1, -1, -1):
            rows = jnp.concatenate([rows] + (yield [(rows, bit)]), axis=0)
        return rows

    def summing(self, make):
        came = yield [(make(1).astype(BF16), 0)]
        rows = make(0) + came[0].astype(F32)
        for bit in range(1, self.bits):
            rows = rows.astype(BF16)
            half = rows.shape[0] // 2
            came = yield [(rows[half:], bit)]
            rows = rows[:half].astype(F32) + came[0].astype(F32)
        return rows

    def own_features(self, block, spot):
        which = spot // block
        place = jnp.zeros_like(which) + lax.axis_index("dp")
        for bit in range(self.bits):
            place = place ^ ((which >> bit & 1) << (self.bits - 1 - bit))
        return place * block + spot % block


def after(field, *others):
    return lax.optimization_barrier((field, *others))[0]


class Line:
    def __init__(self, send, patience):
        self.send = send
        self.patience = patience
        self.prompt = False
        self.count = 0
        self.ending = False
        self.last = None
        self.waiting = []
        self.moving = {}
        self.results = {}

    def add(self, name, begin, *fields):
        self.waiting.append((name, begin, fields))

    def resume(self, name, steps, came):
        try:
            return [(name, steps, steps.send(came))]
        except StopIteration as stop:
            self.results[name] = stop.value
            return []

    def depart(self, leaving):
        for name, steps, hops in leaving:
            due = self.count + 1 + self.patience.get(hops[0][1], 0)
            self.moving[name] = (steps, [self.send(*hop) for hop in hops], due)

    def step(self, field=None, exchange=None, starts=1):
        self.count += 1
        due = [name for name, entry in self.moving.items() if entry[2] <= self.count]
        begun = [self.waiting.pop(0) for _ in range(min(starts, len(self.waiting)))]
        flat = [block for name in due for block in self.moving[name][1]]
        flat += [block for *_, fields in begun for block in fields]
        if field is None:
            flat = list(lax.optimization_barrier(flat)) if flat else flat
        else:
            field, *flat = lax.optimization_barrier((field, *flat))
            came = exchange(field)
        leaving = []
        for name in due:
            steps, blocks, _ = self.moving.pop(name)
            leaving += self.resume(name, steps, [flat.pop(0) for _ in blocks])
        for name, begin, fields in begun:
            leaving += self.resume(name, begin(*[flat.pop(0) for _ in fields]), None)
        self.depart(leaving)
        if field is None:
            return None
        self.begun = [name for name, *_ in begun]
        for name, *_ in begun:
            if self.prompt:
                steps, blocks, due = self.moving[name]
                came, *blocks = lax.optimization_barrier((came, *blocks))
                self.moving[name] = (steps, blocks, due)
        self.last = came
        return came

    def hop(self, name, token):
        steps, blocks, _ = self.moving.pop(name)
        if token is not None:
            blocks = [after(block, token) for block in blocks]
        leaving = self.resume(name, steps, blocks)
        self.depart(leaving)
        return leaving[0][2][0][0] if leaving else self.results[name]

    def need(self, name):
        while name not in self.results:
            self.hop(name, self.last)
        return self.results[name]

    def finish(self):
        token = self.last
        for name in list(self.begun):
            token = self.hop(name, token)
        while self.moving:
            for name in list(self.moving):
                self.hop(name, token)


def per_device(
    tokens,
    text,
    lengths,
    modulation,
    self_qkv,
    self_out,
    cross_query,
    cross_keyvalue,
    cross_out,
    mlp_in,
    mlp_out,
    cotangent,
):
    lay = Layout()
    places = lay.tensor
    rows_here = tokens.shape[1]
    total_rows = rows_here * places
    heads_here = HEADS // places
    columns = heads_here * HEAD_DIM
    wide = padded(columns)
    width = tokens.shape[2]
    block = self_qkv.shape[1]
    me_tensor = lax.axis_index("tensor")
    share = width // places
    half = width // 2
    rows_of = ((0,), (0,))
    over_columns = ((1,), (1,))

    wanted = lay.own_features(block, lax.broadcasted_iota(jnp.int32, (1, width), 1))
    order = (lax.broadcasted_iota(jnp.int32, (width, width), 0) == wanted).astype(BF16)

    def share_order(step):
        first = (me_tensor - step) % places * share
        rows = lax.broadcasted_iota(jnp.int32, (share, width), 0) + first
        return (rows == wanted).astype(BF16)

    shares = [share_order(step) for step in range(places)]

    def exact(left, right, contract):
        return lax.dot_general(
            left,
            right.astype(F32),
            (contract, ((), ())),
            precision=lax.Precision.HIGHEST,
            preferred_element_type=F32,
        )

    def exchange(field, shift):
        starts = starts_at.get(line.count + 1, 0) if forward else 2 if line.ending else 1
        return line.step(field, lambda f: lay.shift(f, shift), starts)

    def spread(field, timed=True):
        came = []
        for k in range(1, places):
            if timed and k == 1:
                came.append(exchange(field, 1))
            else:
                came.append(lay.shift(field, k))
        return [field, jnp.concatenate(came, axis=0) if len(came) > 1 else came[0]]

    def collect(parts):
        own, others = parts
        total = own
        for k in range(1, places):
            leaving = others[(k - 1) * rows_here : k * rows_here].astype(BF16)
            came = exchange(leaving, -1) if k == 1 else lay.shift(leaving, -k)
            total = total + came.astype(F32)
        return total

    def each(parts, weight, contract=((1,), (0,))):
        return [dot(part, weight, contract) for part in parts]

    def low(parts):
        return [part.astype(BF16) for part in parts]

    def join(parts):
        return jnp.concatenate(parts, axis=0)

    def split(field):
        return [field[:rows_here], field[rows_here:]]

    def pack(layer):
        qkv = self_qkv[layer]
        keyval = cross_keyvalue[layer]
        return {
            "qkv": jnp.concatenate([widen(qkv[:, i]) for i in range(3)], axis=1),
            "proj": widen(self_out[layer].T),
            "query": widen(cross_query[layer]),
            "keyval": jnp.concatenate([widen(keyval[:, i]) for i in range(2)], axis=1),
            "cproj": widen(cross_out[layer].T),
            "in": mlp_in[layer],
            "out": mlp_out[layer].T,
        }

    packs = [pack(layer) for layer in range(LAYERS)]
    groups = [
        (layer, names)
        for layer in range(LAYERS)
        for names in (("qkv", "proj"), ("query", "keyval", "cproj"), ("in",), ("out",))
    ]
    line = Line(lay.send, {1: 1})
    place_of = {}
    for index, (layer, names) in enumerate(groups):
        parts = [packs[layer][name] for name in names]
        piece = jnp.concatenate(parts, axis=1) if len(parts) > 1 else parts[0]
        line.add(index, lay.gathering, piece)
        start = 0
        for name, part in zip(names, parts):
            place_of[layer, name] = (index, start, start + part.shape[1])
            start += part.shape[1]
    starts_at = {6: 1, 7: 1, 9: 1, 10: 1, 12: 1}

    def weight(layer, name):
        index, start, stop = place_of[layer, name]
        return line.need(index)[:, start:stop]

    for starts in (1, 0, 1, 0, 1):
        line.step(starts=starts)

    text_rows = jnp.pad(text[0], ((0, LANES - TEXT), (0, 0)))
    text_full = sum(dot(part, at) for part, at in zip([text_rows] + [lay.shift(text_rows, k) for k in range(1, places)], shares))
    text_full = text_full.astype(BF16)
    table = exact(modulation[0].reshape(LAYERS * 6, width), order, ((1,), (0,)))
    table = table.reshape(LAYERS, 6, width)

    def frames(field):
        return field.reshape(-1, rows_here, field.shape[-1])

    def flat(field):
        return field.reshape(-1, field.shape[-1])

    def attend_self(layer, qkv):
        if layer % 2 == 0:
            found = [attend(frames(part), None, (1, rows_here), heads_here) for part in qkv]
            return [flat(one) for one, _ in found], [log for _, log in found]
        period = rows_here // places
        result, log = attend(frames(join(qkv)), None, (places, period), heads_here, period)
        return split(flat(result)), log

    def attend_self_back(layer, qkv, grad, log):
        if layer % 2 == 0:
            return [
                flat(attend_back(frames(a), None, frames(b), c, (1, rows_here), heads_here)[0])
                for a, b, c in zip(qkv, grad, log)
            ]
        period = rows_here // places
        (result,) = attend_back(
            frames(join(qkv)), None, frames(join(grad)), log, (places, period), heads_here, period
        )
        return split(flat(result))

    def attend_cross(queries, keyval):
        found = [
            attend(part[None], keyval[None], (1, part.shape[0]), heads_here, limit=lengths)
            for part in queries
        ]
        return [one[0] for one, _ in found], [log for _, log in found]

    def attend_cross_back(queries, keyval, grad, log):
        found = [
            attend_back(
                a[None], keyval[None], b[None], c, (1, a.shape[0]), heads_here, limit=lengths
            )
            for a, b, c in zip(queries, grad, log)
        ]
        return [one[0] for one, _ in found], sum(two[0] for _, two in found).astype(BF16)

    stream = dot(tokens[0], order)
    memory = []
    forward = True
    for layer in range(LAYERS):
        adaln = table[layer]
        save = {}
        save["unit_one"], save["root_one"] = normalize(stream)
        normed = spread(
            (save["unit_one"] * (1.0 + adaln[1]) + adaln[0]).astype(BF16), layer > 0
        )
        save["normed"] = join(normed)
        save["qkv"] = qkv = low(each(normed, weight(layer, "qkv")))
        attended, save["log_self"] = attend_self(layer, qkv)
        save["attended"] = join(attended)
        save["branch"] = branch = collect(each(attended, weight(layer, "proj"), over_columns))
        stream = stream + adaln[2] * branch
        crossing = spread(stream.astype(BF16))
        save["crossing"] = join(crossing)
        save["queries"] = queries = low(each(crossing, weight(layer, "query")))
        save["keyval"] = keyval = dot(text_full, weight(layer, "keyval")).astype(BF16)
        crossed, save["log_cross"] = attend_cross(queries, keyval)
        save["crossed"] = join(crossed)
        stream = stream + collect(each(crossed, weight(layer, "cproj"), over_columns))
        save["unit_two"], save["root_two"] = normalize(stream)
        inner = spread((save["unit_two"] * (1.0 + adaln[4]) + adaln[3]).astype(BF16))
        save["inner"] = join(inner)
        save["pre"] = pre = each(inner, weight(layer, "in"))
        hidden = low([gelu_tanh(part) for part in pre])
        save["hidden"] = join(hidden)
        save["mlp_branch"] = mlp_branch = collect(each(hidden, weight(layer, "out"), over_columns))
        stream = stream + adaln[5] * mlp_branch
        memory.append(save)
    output = dot(stream.astype(BF16), order, over_columns).astype(BF16)

    def product(*pairs):
        def make(which):
            made = [
                dot(left[:, which * half : (which + 1) * half], right, rows_of)
                for left, right in pairs
            ]
            return made[0] if len(made) == 1 else jnp.concatenate(made, axis=1)
        return lambda: lay.summing(make)

    weights = [
        {name: weight(layer, name) for spot, name in place_of if spot == layer}
        for layer in range(LAYERS)
    ]
    line = Line(lay.send, {})
    line.prompt = True
    forward = False
    grad_stream = dot(cotangent[0], order)
    grad_text = jnp.zeros((LANES, width), F32)
    table_rows = [None] * LAYERS
    for layer in reversed(range(LAYERS)):
        adaln = table[layer]
        kind = weights[layer]
        save = memory[layer]

        grad_gate_two = jnp.sum(grad_stream * save["mlp_branch"], axis=0)
        grad_mlp = spread((adaln[5] * grad_stream).astype(BF16))
        line.add((layer, "out"), product((join(grad_mlp), save["hidden"])))
        grad_pre = [
            jax.vjp(gelu_tanh, pre)[1](dot(part, kind["out"]))[0].astype(BF16)
            for pre, part in zip(save["pre"], grad_mlp)
        ]
        line.add((layer, "in"), product((save["inner"], join(grad_pre))))
        grad_inner = collect(each(grad_pre, kind["in"], over_columns))
        grad_shift_two = jnp.sum(grad_inner, axis=0)
        grad_scale_two = jnp.sum(grad_inner * save["unit_two"], axis=0)
        grad_stream = grad_stream + norm_back(
            grad_inner * (1.0 + adaln[4]), save["unit_two"], save["root_two"]
        )

        grad_crossed = spread(grad_stream.astype(BF16))
        grad_catt = low(each(grad_crossed, kind["cproj"]))
        grad_cq, grad_keyval = attend_cross_back(
            save["queries"], save["keyval"], grad_catt, save["log_cross"]
        )
        line.add(
            (layer, "cross"),
            product(
                (save["crossing"], join(grad_cq)),
                (text_full, grad_keyval),
                (join(grad_crossed), save["crossed"]),
            ),
        )
        grad_stream = grad_stream + collect(each(grad_cq, kind["query"], over_columns))
        grad_text = grad_text + dot(grad_keyval, kind["keyval"], over_columns)

        grad_gate_one = jnp.sum(grad_stream * save["branch"], axis=0)
        grad_branch = spread((adaln[2] * grad_stream).astype(BF16))
        line.add((layer, "proj"), product((join(grad_branch), save["attended"])))
        grad_att = low(each(grad_branch, kind["proj"]))
        grad_qkv = attend_self_back(layer, save["qkv"], grad_att, save["log_self"])
        line.add(
            (layer, "self"),
            product((save["normed"], join(grad_qkv))),
        )
        line.ending = layer == 0
        grad_normed = collect(each(grad_qkv, kind["qkv"], over_columns))
        grad_shift_one = jnp.sum(grad_normed, axis=0)
        grad_scale_one = jnp.sum(grad_normed * save["unit_one"], axis=0)
        grad_stream = grad_stream + norm_back(
            grad_normed * (1.0 + adaln[1]), save["unit_one"], save["root_one"]
        )
        table_rows[layer] = jnp.stack(
            [
                grad_shift_one,
                grad_scale_one,
                grad_gate_one,
                grad_shift_two,
                grad_scale_two,
                grad_gate_two,
            ]
        )
    line.finish()

    def apart(field, first, count):
        return jnp.stack(
            [field[:, i * wide : i * wide + columns] for i in range(first, first + count)], axis=1
        )

    text_parts = [exact(grad_text[:TEXT], at, over_columns) for at in shares]
    text_grad = text_parts[0]
    for k in range(1, places):
        text_grad = text_grad + lay.shift(text_parts[k], -k)
    table_grad = exact(jnp.stack(table_rows).reshape(LAYERS * 6, width), order, over_columns)
    if places == 2:
        table_grad = table_grad + lay.shift(table_grad, 1)
    else:
        table_grad = lax.psum(table_grad, "tensor")
    selfs = [line.results[layer, "self"] for layer in range(LAYERS)]
    crosses = [line.results[layer, "cross"] for layer in range(LAYERS)]
    return (
        output[None],
        exact(grad_stream, order, over_columns)[None],
        text_grad[None],
        table_grad.reshape(LAYERS, 6, width)[None],
        jnp.stack([apart(one, 0, 3) for one in selfs]),
        jnp.stack([line.results[layer, "proj"][:, :columns].T for layer in range(LAYERS)]),
        jnp.stack([one[:, :columns] for one in crosses]),
        jnp.stack([apart(one, 1, 2) for one in crosses]),
        jnp.stack([one[:, 3 * wide : 3 * wide + columns].T for one in crosses]),
        jnp.stack([line.results[layer, "in"] for layer in range(LAYERS)]),
        jnp.stack([line.results[layer, "out"].T for layer in range(LAYERS)]),
    )


def solution(mesh):
    return jax.shard_map(
        per_device,
        mesh=mesh,
        in_specs=(
            P("dp", "tensor", None),
            P("dp", None, "tensor"),
            P("dp"),
            P("dp", None, None, None),
            P(None, "dp", None, "tensor"),
            P(None, "tensor", "dp"),
            P(None, "dp", "tensor"),
            P(None, "dp", None, "tensor"),
            P(None, "tensor", "dp"),
            P(None, "dp", "tensor"),
            P(None, "tensor", "dp"),
            P("dp", "tensor", None),
        ),
        out_specs=(
            P("dp", "tensor", None),
            P("dp", "tensor", None),
            P("dp", None, "tensor"),
            P("dp", None, None, None),
            P(None, "dp", None, "tensor"),
            P(None, "tensor", "dp"),
            P(None, "dp", "tensor"),
            P(None, "dp", None, "tensor"),
            P(None, "tensor", "dp"),
            P(None, "dp", "tensor"),
            P(None, "tensor", "dp"),
        ),
        check_vma=False,
    )
```

```python
import jax
import jax.numpy as jnp
from jax import lax
from jax.experimental import pallas as pl
from jax.experimental.pallas import tpu as pltpu
from jax.sharding import PartitionSpec as P

HEADS = 16
HEAD_DIM = 72
TEXT = 120
PATCH = 256
LAYERS = 2
LANES = 128

EPSILON = 1e-06
NEG_FILL = -1e30
F32 = jnp.float32
BF16 = jnp.bfloat16


def normalize(stream):
    center = stream - jnp.mean(stream, axis=-1, keepdims=True)
    root = lax.rsqrt(jnp.mean(center * center, axis=-1, keepdims=True) + EPSILON)
    return (center * root, root)


def norm_back(grad, unit, root):
    return root * (
        grad
        - jnp.mean(grad, axis=-1, keepdims=True)
        - unit * jnp.mean(grad * unit, axis=-1, keepdims=True)
    )


def gelu_tanh(field):
    return jax.nn.gelu(field, approximate=True)


def dot(left, right, contract=((1,), (0,))):
    return lax.dot_general(left, right, (contract, ((), ())), preferred_element_type=F32)


def padded(width):
    return -(-width // LANES) * LANES


def widen(field):
    extra = padded(field.shape[-1]) - field.shape[-1]
    if extra == 0:
        return field
    return jnp.pad(field, [(0, 0)] * (field.ndim - 1) + [(0, extra)])


def head_window(head):
    first = head * HEAD_DIM
    low = first // LANES * LANES
    high = padded(first + HEAD_DIM)
    lane = lax.broadcasted_iota(jnp.int32, (1, high - low), 1) + low
    return low, high, (lane >= first) & (lane < first + HEAD_DIM)


def hide(scores, limit_ref, period):
    if limit_ref is not None:
        key = lax.broadcasted_iota(jnp.int32, scores.shape, 1)
        return jnp.where(key < limit_ref[0], scores, NEG_FILL)
    if period is not None:
        row = lax.broadcasted_iota(jnp.int32, scores.shape, 0)
        key = lax.broadcasted_iota(jnp.int32, scores.shape, 1)
        return jnp.where(lax.rem(row, period) == lax.rem(key, period), scores, NEG_FILL)
    return scores


def attend_kernel(heads, period, limited, *refs):
    limit_ref = refs[0] if limited else None
    q_ref, k_ref, v_ref, out_ref, log_ref, held = refs[1 if limited else 0 :]
    scaling = HEAD_DIM ** (-0.5)
    held[...] = jnp.zeros_like(held)
    rows = held.shape[0]
    lane = lax.broadcasted_iota(jnp.int32, (rows, LANES), 1)
    logs = jnp.zeros((rows, LANES), F32)

    def take(ref, low, high):
        field = ref[:, :, low:high]
        return field.reshape(field.shape[0] * field.shape[1], high - low)

    for head in range(heads):
        low, high, inside = head_window(head)
        keep = inside.astype(F32).astype(BF16)
        scores = dot(take(q_ref, low, high) * keep, take(k_ref, low, high), ((1,), (1,)))
        scores = hide(scores * scaling, limit_ref, period)
        top = jnp.max(scores, axis=1, keepdims=True)
        weights = jnp.exp(scores - top)
        total = jnp.sum(weights, axis=1, keepdims=True)
        weights = (weights * (1.0 / total)).astype(BF16)
        result = dot(weights, take(v_ref, low, high))
        held[:, low:high] = jnp.where(inside, result, held[:, low:high])
        logs = jnp.where(lane == head, top + jnp.log(total), logs)
    out_ref[...] = held[...].astype(BF16).reshape(out_ref.shape)
    log_ref[...] = logs.reshape(log_ref.shape)


def attend_back_kernel(heads, period, limited, packed, *refs):
    limit_ref = refs[0] if limited else None
    refs = refs[1 if limited else 0 :]
    q_ref, k_ref, v_ref, grad_ref, log_ref, *outs, q_held, k_held, v_held = refs
    scaling = HEAD_DIM ** (-0.5)
    for held in (q_held, k_held, v_held):
        held[...] = jnp.zeros_like(held)
    rows = q_held.shape[0]
    lane = lax.broadcasted_iota(jnp.int32, (rows, LANES), 1)

    def take(ref, low, high):
        field = ref[:, :, low:high]
        return field.reshape(field.shape[0] * field.shape[1], high - low)

    for head in range(heads):
        low, high, inside = head_window(head)
        keep = inside.astype(F32).astype(BF16)
        queries = take(q_ref, low, high)
        keys = take(k_ref, low, high)
        grads = take(grad_ref, low, high)
        scores = dot(queries * keep, keys, ((1,), (1,))) * scaling
        scores = hide(scores, limit_ref, period)
        logs = jnp.where(lane == head, take(log_ref, 0, LANES), 0.0)
        probs = jnp.exp(scores - jnp.sum(logs, axis=1, keepdims=True))
        grad_probs = dot(grads * keep, take(v_ref, low, high), ((1,), (1,)))
        mean = jnp.sum(probs * grad_probs, axis=1, keepdims=True)
        grad_scores = (probs * (grad_probs - mean)).astype(BF16)
        first = ((0,), (0,))
        for held, value in (
            (q_held, dot(grad_scores, keys) * scaling),
            (k_held, dot(grad_scores, queries, first) * scaling),
            (v_held, dot(probs.astype(BF16), grads, first)),
        ):
            held[:, low:high] = jnp.where(inside, value, held[:, low:high])
    width = q_held.shape[1]
    query_out = outs[0]
    others = outs[0] if packed else outs[1]
    start = width if packed else 0
    spot = query_out.shape[:2] + (width,)
    query_out[:, :, :width] = q_held[...].astype(BF16).reshape(spot)
    spot = others.shape[:2] + (width,)
    others[:, :, start : start + width] = k_held[...].astype(others.dtype).reshape(spot)
    others[:, :, start + width :] = v_held[...].astype(others.dtype).reshape(spot)


def kernel_cost(units, heads, rows, keys, products):
    area = units * heads * rows * keys
    return pl.CostEstimate(
        flops=products * 2 * area * 256,
        transcendentals=area,
        bytes_accessed=units * (4 * rows + 2 * keys) * padded(heads * HEAD_DIM) * 2,
    )


def attend_parts(query, keyval, unit, heads):
    wide = padded(heads * HEAD_DIM)
    frames, rows = query.shape[:2]
    units = (frames // unit[0]) * (rows // unit[1])
    across = frames // unit[0]

    def at(u, column):
        return (u % across, u // across, column)

    own = pl.BlockSpec((*unit, wide), lambda u, *_: at(u, 0))
    if keyval is None:
        arrays = [query] * 3
        rest = [
            pl.BlockSpec((*unit, wide), lambda u, *_: at(u, 1)),
            pl.BlockSpec((*unit, wide), lambda u, *_: at(u, 2)),
        ]
        keys = unit[0] * unit[1]
    else:
        arrays = [query, keyval, keyval]
        keys = keyval.shape[1]
        rest = [
            pl.BlockSpec((1, keys, wide), lambda u, *_: (0, 0, 0)),
            pl.BlockSpec((1, keys, wide), lambda u, *_: (0, 0, 1)),
        ]
    logs = pl.BlockSpec((*unit, LANES), lambda u, *_: at(u, 0))
    packed = pl.BlockSpec((*unit, 3 * wide), lambda u, *_: at(u, 0))
    return arrays, [own, *rest], own, logs, packed, units, keys, wide


def attend(query, keyval, unit, heads, period=None, limit=None):
    arrays, specs, own, logs, _, units, keys, wide = attend_parts(query, keyval, unit, heads)
    limited = limit is not None
    rows = unit[0] * unit[1]
    return pl.pallas_call(
        lambda *refs: attend_kernel(heads, period, limited, *refs),
        out_shape=(
            jax.ShapeDtypeStruct((*query.shape[:2], wide), BF16),
            jax.ShapeDtypeStruct((*query.shape[:2], LANES), F32),
        ),
        grid_spec=pltpu.PrefetchScalarGridSpec(
            num_scalar_prefetch=1 if limited else 0,
            grid=(units,),
            in_specs=specs,
            out_specs=(own, logs),
            scratch_shapes=[pltpu.VMEM((rows, wide), F32)],
        ),
        cost_estimate=kernel_cost(units, heads, rows, keys, 2),
        name="attend",
    )(*([limit] if limited else []), *arrays)


def attend_back(query, keyval, grad, log, unit, heads, period=None, limit=None):
    arrays, specs, own, logs, packed, units, keys, wide = attend_parts(query, keyval, unit, heads)
    rows = unit[0] * unit[1]
    if keyval is None:
        out_shape = (jax.ShapeDtypeStruct(query.shape, BF16),)
        out_specs = (packed,)
    else:
        assert units == 1
        out_shape = (
            jax.ShapeDtypeStruct(query.shape, BF16),
            jax.ShapeDtypeStruct(keyval.shape, F32),
        )
        out_specs = (own, pl.BlockSpec((1, keys, 2 * wide), lambda u, *_: (0, 0, 0)))
    limited = limit is not None
    return pl.pallas_call(
        lambda *refs: attend_back_kernel(heads, period, limited, keyval is None, *refs),
        out_shape=out_shape,
        grid_spec=pltpu.PrefetchScalarGridSpec(
            num_scalar_prefetch=1 if limited else 0,
            grid=(units,),
            in_specs=[*specs, own, logs],
            out_specs=out_specs,
            scratch_shapes=[
                pltpu.VMEM((rows, wide), F32),
                pltpu.VMEM((keys, wide), F32),
                pltpu.VMEM((keys, wide), F32),
            ],
        ),
        cost_estimate=kernel_cost(units, heads, rows, keys, 5),
        name="attend_back",
    )(*([limit] if limited else []), *arrays, grad, log)


class Layout:
    def __init__(self):
        self.dp = lax.axis_size("dp")
        self.bits = self.dp.bit_length() - 1
        self.tensor = lax.axis_size("tensor")

    def send(self, field, bit):
        return lax.ppermute(field, "dp", [(place, place ^ (1 << bit)) for place in range(self.dp)])

    def shift(self, field, step):
        size = self.tensor
        return lax.ppermute(field, "tensor", [(i, (i + step) % size) for i in range(size)])

    def gathering(self, rows):
        for bit in range(self.bits - 1, -1, -1):
            rows = jnp.concatenate([rows] + (yield [(rows, bit)]), axis=0)
        return rows

    def summing(self, make):
        came = yield [(make(1).astype(BF16), 0)]
        rows = make(0) + came[0].astype(F32)
        for bit in range(1, self.bits):
            rows = rows.astype(BF16)
            half = rows.shape[0] // 2
            came = yield [(rows[half:], bit)]
            rows = rows[:half].astype(F32) + came[0].astype(F32)
        return rows

    def own_features(self, block, spot):
        which = spot // block
        place = jnp.zeros_like(which) + lax.axis_index("dp")
        for bit in range(self.bits):
            place = place ^ ((which >> bit & 1) << (self.bits - 1 - bit))
        return place * block + spot % block


def after(field, *others):
    return lax.optimization_barrier((field, *others))[0]


class Line:
    def __init__(self, send, patience):
        self.send = send
        self.patience = patience
        self.prompt = False
        self.count = 0
        self.ending = False
        self.last = None
        self.waiting = []
        self.moving = {}
        self.results = {}

    def add(self, name, begin, *fields):
        self.waiting.append((name, begin, fields))

    def resume(self, name, steps, came):
        try:
            return [(name, steps, steps.send(came))]
        except StopIteration as stop:
            self.results[name] = stop.value
            return []

    def depart(self, leaving):
        for name, steps, hops in leaving:
            due = self.count + 1 + self.patience.get(hops[0][1], 0)
            self.moving[name] = (steps, [self.send(*hop) for hop in hops], due)

    def step(self, field=None, exchange=None, starts=1):
        self.count += 1
        due = [name for name, entry in self.moving.items() if entry[2] <= self.count]
        begun = [self.waiting.pop(0) for _ in range(min(starts, len(self.waiting)))]
        flat = [block for name in due for block in self.moving[name][1]]
        flat += [block for *_, fields in begun for block in fields]
        if field is None:
            flat = list(lax.optimization_barrier(flat)) if flat else flat
        else:
            field, *flat = lax.optimization_barrier((field, *flat))
            came = exchange(field)
        leaving = []
        for name in due:
            steps, blocks, _ = self.moving.pop(name)
            leaving += self.resume(name, steps, [flat.pop(0) for _ in blocks])
        for name, begin, fields in begun:
            leaving += self.resume(name, begin(*[flat.pop(0) for _ in fields]), None)
        self.depart(leaving)
        if field is None:
            return None
        self.begun = [name for name, *_ in begun]
        for name, *_ in begun:
            if self.prompt:
                steps, blocks, due = self.moving[name]
                came, *blocks = lax.optimization_barrier((came, *blocks))
                self.moving[name] = (steps, blocks, due)
        self.last = came
        return came

    def hop(self, name, token):
        steps, blocks, _ = self.moving.pop(name)
        if token is not None:
            blocks = [after(block, token) for block in blocks]
        leaving = self.resume(name, steps, blocks)
        self.depart(leaving)
        return leaving[0][2][0][0] if leaving else self.results[name]

    def need(self, name):
        while name not in self.results:
            self.hop(name, self.last)
        return self.results[name]

    def finish(self):
        token = self.last
        for name in list(self.begun):
            token = self.hop(name, token)
        while self.moving:
            for name in list(self.moving):
                self.hop(name, token)


def per_device(
    tokens,
    text,
    lengths,
    modulation,
    self_qkv,
    self_out,
    cross_query,
    cross_keyvalue,
    cross_out,
    mlp_in,
    mlp_out,
    cotangent,
):
    lay = Layout()
    places = lay.tensor
    rows_here = tokens.shape[1]
    total_rows = rows_here * places
    heads_here = HEADS // places
    columns = heads_here * HEAD_DIM
    wide = padded(columns)
    width = tokens.shape[2]
    block = self_qkv.shape[1]
    me_tensor = lax.axis_index("tensor")
    share = width // places
    half = width // 2
    rows_of = ((0,), (0,))
    over_columns = ((1,), (1,))

    wanted = lay.own_features(block, lax.broadcasted_iota(jnp.int32, (1, width), 1))
    order = (lax.broadcasted_iota(jnp.int32, (width, width), 0) == wanted).astype(BF16)

    def share_order(step):
        first = (me_tensor - step) % places * share
        rows = lax.broadcasted_iota(jnp.int32, (share, width), 0) + first
        return (rows == wanted).astype(BF16)

    shares = [share_order(step) for step in range(places)]

    def exact(left, right, contract):
        return lax.dot_general(
            left,
            right.astype(F32),
            (contract, ((), ())),
            precision=lax.Precision.HIGHEST,
            preferred_element_type=F32,
        )

    def exchange(field, shift):
        starts = starts_at.get(line.count + 1, 0) if forward else 2 if line.ending else 1
        return line.step(field, lambda f: lay.shift(f, shift), starts)

    def spread(field, timed=True):
        came = []
        for k in range(1, places):
            if timed and k == 1:
                came.append(exchange(field, 1))
            else:
                came.append(lay.shift(field, k))
        return [field, jnp.concatenate(came, axis=0) if len(came) > 1 else came[0]]

    def collect(parts):
        own, others = parts
        total = own
        for k in range(1, places):
            leaving = others[(k - 1) * rows_here : k * rows_here].astype(BF16)
            came = exchange(leaving, -1) if k == 1 else lay.shift(leaving, -k)
            total = total + came.astype(F32)
        return total

    def each(parts, weight, contract=((1,), (0,))):
        return [dot(part, weight, contract) for part in parts]

    def low(parts):
        return [part.astype(BF16) for part in parts]

    def join(parts):
        return jnp.concatenate(parts, axis=0)

    def split(field):
        return [field[:rows_here], field[rows_here:]]

    def pack(layer):
        qkv = self_qkv[layer]
        keyval = cross_keyvalue[layer]
        return {
            "qkv": jnp.concatenate([widen(qkv[:, i]) for i in range(3)], axis=1),
            "proj": widen(self_out[layer].T),
            "query": widen(cross_query[layer]),
            "keyval": jnp.concatenate([widen(keyval[:, i]) for i in range(2)], axis=1),
            "cproj": widen(cross_out[layer].T),
            "in": mlp_in[layer],
            "out": mlp_out[layer].T,
        }

    packs = [pack(layer) for layer in range(LAYERS)]
    groups = [
        (layer, names)
        for layer in range(LAYERS)
        for names in (("qkv", "proj"), ("query", "keyval", "cproj"), ("in",), ("out",))
    ]
    line = Line(lay.send, {1: 1})
    place_of = {}
    for index, (layer, names) in enumerate(groups):
        parts = [packs[layer][name] for name in names]
        piece = jnp.concatenate(parts, axis=1) if len(parts) > 1 else parts[0]
        line.add(index, lay.gathering, piece)
        start = 0
        for name, part in zip(names, parts):
            place_of[layer, name] = (index, start, start + part.shape[1])
            start += part.shape[1]
    starts_at = {6: 1, 7: 1, 9: 1, 11: 1, 12: 1}

    def weight(layer, name):
        index, start, stop = place_of[layer, name]
        return line.need(index)[:, start:stop]

    for starts in (1, 0, 1, 0, 1):
        line.step(starts=starts)

    text_rows = jnp.pad(text[0], ((0, LANES - TEXT), (0, 0)))
    text_full = sum(dot(part, at) for part, at in zip([text_rows] + [lay.shift(text_rows, k) for k in range(1, places)], shares))
    text_full = text_full.astype(BF16)
    table = exact(modulation[0].reshape(LAYERS * 6, width), order, ((1,), (0,)))
    table = table.reshape(LAYERS, 6, width)

    def frames(field):
        return field.reshape(-1, rows_here, field.shape[-1])

    def flat(field):
        return field.reshape(-1, field.shape[-1])

    def attend_self(layer, qkv):
        if layer % 2 == 0:
            found = [attend(frames(part), None, (1, rows_here), heads_here) for part in qkv]
            return [flat(one) for one, _ in found], [log for _, log in found]
        period = rows_here // places
        result, log = attend(frames(join(qkv)), None, (places, period), heads_here, period)
        return split(flat(result)), log

    def attend_self_back(layer, qkv, grad, log):
        if layer % 2 == 0:
            return [
                flat(attend_back(frames(a), None, frames(b), c, (1, rows_here), heads_here)[0])
                for a, b, c in zip(qkv, grad, log)
            ]
        period = rows_here // places
        (result,) = attend_back(
            frames(join(qkv)), None, frames(join(grad)), log, (places, period), heads_here, period
        )
        return split(flat(result))

    def attend_cross(queries, keyval):
        found = [
            attend(part[None], keyval[None], (1, part.shape[0]), heads_here, limit=lengths)
            for part in queries
        ]
        return [one[0] for one, _ in found], [log for _, log in found]

    def attend_cross_back(queries, keyval, grad, log):
        found = [
            attend_back(
                a[None], keyval[None], b[None], c, (1, a.shape[0]), heads_here, limit=lengths
            )
            for a, b, c in zip(queries, grad, log)
        ]
        return [one[0] for one, _ in found], sum(two[0] for _, two in found).astype(BF16)

    stream = dot(tokens[0], order)
    memory = []
    forward = True
    for layer in range(LAYERS):
        adaln = table[layer]
        save = {}
        save["unit_one"], save["root_one"] = normalize(stream)
        normed = spread(
            (save["unit_one"] * (1.0 + adaln[1]) + adaln[0]).astype(BF16), layer > 0
        )
        save["normed"] = join(normed)
        save["qkv"] = qkv = low(each(normed, weight(layer, "qkv")))
        attended, save["log_self"] = attend_self(layer, qkv)
        save["attended"] = join(attended)
        save["branch"] = branch = collect(each(attended, weight(layer, "proj"), over_columns))
        stream = stream + adaln[2] * branch
        crossing = spread(stream.astype(BF16))
        save["crossing"] = join(crossing)
        save["queries"] = queries = low(each(crossing, weight(layer, "query")))
        save["keyval"] = keyval = dot(text_full, weight(layer, "keyval")).astype(BF16)
        crossed, save["log_cross"] = attend_cross(queries, keyval)
        save["crossed"] = join(crossed)
        stream = stream + collect(each(crossed, weight(layer, "cproj"), over_columns))
        save["unit_two"], save["root_two"] = normalize(stream)
        inner = spread((save["unit_two"] * (1.0 + adaln[4]) + adaln[3]).astype(BF16))
        save["inner"] = join(inner)
        save["pre"] = pre = each(inner, weight(layer, "in"))
        hidden = low([gelu_tanh(part) for part in pre])
        save["hidden"] = join(hidden)
        save["mlp_branch"] = mlp_branch = collect(each(hidden, weight(layer, "out"), over_columns))
        stream = stream + adaln[5] * mlp_branch
        memory.append(save)
    output = dot(stream.astype(BF16), order, over_columns).astype(BF16)

    def product(*pairs):
        def make(which):
            made = [
                dot(left[:, which * half : (which + 1) * half], right, rows_of)
                for left, right in pairs
            ]
            return made[0] if len(made) == 1 else jnp.concatenate(made, axis=1)
        return lambda: lay.summing(make)

    weights = [
        {name: weight(layer, name) for spot, name in place_of if spot == layer}
        for layer in range(LAYERS)
    ]
    line = Line(lay.send, {})
    line.prompt = True
    forward = False
    grad_stream = dot(cotangent[0], order)
    grad_text = jnp.zeros((LANES, width), F32)
    table_rows = [None] * LAYERS
    for layer in reversed(range(LAYERS)):
        adaln = table[layer]
        kind = weights[layer]
        save = memory[layer]

        grad_gate_two = jnp.sum(grad_stream * save["mlp_branch"], axis=0)
        grad_mlp = spread((adaln[5] * grad_stream).astype(BF16))
        line.add((layer, "out"), product((join(grad_mlp), save["hidden"])))
        grad_pre = [
            jax.vjp(gelu_tanh, pre)[1](dot(part, kind["out"]))[0].astype(BF16)
            for pre, part in zip(save["pre"], grad_mlp)
        ]
        line.add((layer, "in"), product((save["inner"], join(grad_pre))))
        grad_inner = collect(each(grad_pre, kind["in"], over_columns))
        grad_shift_two = jnp.sum(grad_inner, axis=0)
        grad_scale_two = jnp.sum(grad_inner * save["unit_two"], axis=0)
        grad_stream = grad_stream + norm_back(
            grad_inner * (1.0 + adaln[4]), save["unit_two"], save["root_two"]
        )

        grad_crossed = spread(grad_stream.astype(BF16))
        grad_catt = low(each(grad_crossed, kind["cproj"]))
        grad_cq, grad_keyval = attend_cross_back(
            save["queries"], save["keyval"], grad_catt, save["log_cross"]
        )
        line.add(
            (layer, "cross"),
            product(
                (save["crossing"], join(grad_cq)),
                (text_full, grad_keyval),
                (join(grad_crossed), save["crossed"]),
            ),
        )
        grad_stream = grad_stream + collect(each(grad_cq, kind["query"], over_columns))
        grad_text = grad_text + dot(grad_keyval, kind["keyval"], over_columns)

        grad_gate_one = jnp.sum(grad_stream * save["branch"], axis=0)
        grad_branch = spread((adaln[2] * grad_stream).astype(BF16))
        line.add((layer, "proj"), product((join(grad_branch), save["attended"])))
        grad_att = low(each(grad_branch, kind["proj"]))
        grad_qkv = attend_self_back(layer, save["qkv"], grad_att, save["log_self"])
        line.add(
            (layer, "self"),
            product((save["normed"], join(grad_qkv))),
        )
        line.ending = layer == 0
        grad_normed = collect(each(grad_qkv, kind["qkv"], over_columns))
        grad_shift_one = jnp.sum(grad_normed, axis=0)
        grad_scale_one = jnp.sum(grad_normed * save["unit_one"], axis=0)
        grad_stream = grad_stream + norm_back(
            grad_normed * (1.0 + adaln[1]), save["unit_one"], save["root_one"]
        )
        table_rows[layer] = jnp.stack(
            [
                grad_shift_one,
                grad_scale_one,
                grad_gate_one,
                grad_shift_two,
                grad_scale_two,
                grad_gate_two,
            ]
        )
    line.finish()

    def apart(field, first, count):
        return jnp.stack(
            [field[:, i * wide : i * wide + columns] for i in range(first, first + count)], axis=1
        )

    text_parts = [exact(grad_text[:TEXT], at, over_columns) for at in shares]
    text_grad = text_parts[0]
    for k in range(1, places):
        text_grad = text_grad + lay.shift(text_parts[k], -k)
    table_grad = exact(jnp.stack(table_rows).reshape(LAYERS * 6, width), order, over_columns)
    if places == 2:
        table_grad = table_grad + lay.shift(table_grad, 1)
    else:
        table_grad = lax.psum(table_grad, "tensor")
    selfs = [line.results[layer, "self"] for layer in range(LAYERS)]
    crosses = [line.results[layer, "cross"] for layer in range(LAYERS)]
    return (
        output[None],
        exact(grad_stream, order, over_columns)[None],
        text_grad[None],
        table_grad.reshape(LAYERS, 6, width)[None],
        jnp.stack([apart(one, 0, 3) for one in selfs]),
        jnp.stack([line.results[layer, "proj"][:, :columns].T for layer in range(LAYERS)]),
        jnp.stack([one[:, :columns] for one in crosses]),
        jnp.stack([apart(one, 1, 2) for one in crosses]),
        jnp.stack([one[:, 3 * wide : 3 * wide + columns].T for one in crosses]),
        jnp.stack([line.results[layer, "in"] for layer in range(LAYERS)]),
        jnp.stack([line.results[layer, "out"].T for layer in range(LAYERS)]),
    )


def solution(mesh):
    return jax.shard_map(
        per_device,
        mesh=mesh,
        in_specs=(
            P("dp", "tensor", None),
            P("dp", None, "tensor"),
            P("dp"),
            P("dp", None, None, None),
            P(None, "dp", None, "tensor"),
            P(None, "tensor", "dp"),
            P(None, "dp", "tensor"),
            P(None, "dp", None, "tensor"),
            P(None, "tensor", "dp"),
            P(None, "dp", "tensor"),
            P(None, "tensor", "dp"),
            P("dp", "tensor", None),
        ),
        out_specs=(
            P("dp", "tensor", None),
            P("dp", "tensor", None),
            P("dp", None, "tensor"),
            P("dp", None, None, None),
            P(None, "dp", None, "tensor"),
            P(None, "tensor", "dp"),
            P(None, "dp", "tensor"),
            P(None, "dp", None, "tensor"),
            P(None, "tensor", "dp"),
            P(None, "dp", "tensor"),
            P(None, "tensor", "dp"),
        ),
        check_vma=False,
    )
```
